32 devices in a mesh: dp: 8 (over z, y), tensor: 4 (over x, core).
Axes of the slice: x: 2, y: 2, z: 4, core: 2. Of those that a mesh axis runs over, the one named last changes fastest.
Arguments:
- signal: bfloat16 [26112, 512], P('dp', 'tensor'), may hold values from -6 to 6
- horizon: int32 [32], P('dp'), may hold values from 96 to 720, as said below
- down_a: bfloat16 [6144, 512], P('dp', 'tensor'), may hold values from -0.078125 to 0.078125
- iso_a: bfloat16 [34816, 512], P('dp', 'tensor'), may hold values from -0.046875 to 0.046875
- up_a: bfloat16 [512, 12, 512], P('dp', None, 'tensor'), may hold values from -0.25 to 0.25
- down_b: bfloat16 [8192, 512], P('dp', 'tensor'), may hold values from -0.0625 to 0.0625
- iso_b: bfloat16 [26112, 512], P('dp', 'tensor'), may hold values from -0.0546875 to 0.0546875
- up_b: bfloat16 [512, 16, 512], P('dp', None, 'tensor'), may hold values from -0.25 to 0.25
- merge_w: bfloat16 [1024, 512], P('dp', 'tensor'), may hold values from -0.1875 to 0.1875
- ff_in: bfloat16 [512, 2048], P(None, 'tensor'), may hold values from -0.25 to 0.25
- ff_out: bfloat16 [2048, 512], P('tensor'), may hold values from -0.125 to 0.125
- norm_gain: float32 [512], P('tensor'), may hold values from 0.1 to 1.9
- norm_bias: float32 [512], P('tensor'), may hold values from -4 to 4
- first_gain: float32 [512], P('tensor'), may hold values from 0.1 to 1.9
- first_bias: float32 [512], P('tensor'), may hold values from -4 to 4
- last_gain: float32 [512], P('tensor'), may hold values from 0.1 to 1.9
- last_bias: float32 [512], P('tensor'), may hold values from -4 to 4
- cotangent: bfloat16 [26112, 512], P('dp', 'tensor'), may hold values from -6 to 6
Outputs:
- series_out: bfloat16 [26112, 512], P('dp', 'tensor')
- grad_input: float32 [26112, 512], P('dp', 'tensor')
- grad_down_a: float32 [6144, 512], P('dp', 'tensor')
- grad_iso_a: float32 [34816, 512], P('dp', 'tensor')
- grad_up_a: float32 [512, 12, 512], P('dp', None, 'tensor')
- grad_down_b: float32 [8192, 512], P('dp', 'tensor')
- grad_iso_b: float32 [26112, 512], P('dp', 'tensor')
- grad_up_b: float32 [512, 16, 512], P('dp', None, 'tensor')
- grad_merge: float32 [1024, 512], P('dp', 'tensor')
- grad_ff_in: float32 [512, 2048], P(None, 'tensor')
- grad_ff_out: float32 [2048, 512], P('tensor')
- grad_norm_gain: float32 [512], P('tensor')
- grad_norm_bias: float32 [512], P('tensor')
- grad_first_gain: float32 [512], P('tensor')
- grad_first_bias: float32 [512], P('tensor')
- grad_last_gain: float32 [512], P('tensor')
- grad_last_bias: float32 [512], P('tensor')
The draws below stay inside these ranges and needn't reach their ends.
Inputs may be any that keep to these rules, and one draw needn't show every extreme that they name: Each series' horizon is one of 96, 192, 336 and 720; some series has 720.
All inputs are finite; a program needn't handle non-finite values.
Results may differ from the reference program's by a relative error of at most 0.014.
Values may be sent and summed in bfloat16 or wider, within the bound.
No kernel may reach another device: no remote copies, remote signals or barrier semaphores. Data moves between devices by JAX's collectives and lax.ppermute only.
A program may use at most 384 MiB of HBM per device.

```python
import jax
import jax.numpy as jnp
from jax import lax

D = 512
FF = 2048
SA = 12
SB = 16
IN_LEN = 96
HORIZON = 720
L = 816
MA = 68
MB = 51
SERIES = 32


def draw_horizon(key, part):
    first_key, second_key = jax.random.split(jax.random.fold_in(key, 17))
    levels = jnp.array([2, 4, 7, 15], dtype=jnp.int32)
    picks = jax.random.randint(first_key, (SERIES,), 0, 4)
    longest = jax.random.randint(second_key, (), 0, SERIES)
    picks = jnp.where(jnp.arange(SERIES, dtype=jnp.int32) == longest, 3, picks)
    return levels[picks] * HORIZON // 15


def block_levels(own_key, shape, cuts, smallest, top_value):
    level, own = 1.0, jax.random.fold_in(own_key, 6)
    for axis_at, parts in cuts:
        draws = jnp.exp(jax.random.uniform(jax.random.fold_in(own, axis_at), (parts,), jnp.float32, smallest / len(cuts), top_value / len(cuts)))
        level = level * jnp.repeat(draws, shape[axis_at] // parts).reshape([-1 if axis == axis_at else 1 for axis in range(len(shape))])
    return level


def noise(rng, dims, scale, bound, cuts=(), held_as=jnp.bfloat16):
    values = jax.random.normal(rng, dims, jnp.float32) * scale
    if len(cuts) > 0:
        values = block_levels(rng, dims, cuts, -0.22, 0.18) * values
    return jnp.clip(values, min=-bound, max=bound).astype(held_as)


def setup_inputs(seed: int = 0) -> dict:
    splits = jax.random.split(jax.random.key(seed), 19)
    return {
        "signal": noise(splits[0], (SERIES * L, D), 1.0, 6.0, ((0, 8), (1, 4))),
        "horizon": draw_horizon(jax.random.fold_in(splits[18], 71), 0),
        "down_a": noise(splits[2], (SA * D, D), (SA * D) ** -0.5, 0.078125, ((0, 8), (1, 4))),
        "iso_a": noise(splits[3], (MA * D, D), (MA * D // 2) ** -0.5, 0.046875, ((0, 8), (1, 4))),
        "up_a": noise(splits[4], (D, SA, D), D ** -0.5, 0.25, ((0, 8), (2, 4))),
        "down_b": noise(splits[5], (SB * D, D), (SB * D) ** -0.5, 0.0625, ((0, 8), (1, 4))),
        "iso_b": noise(splits[6], (MB * D, D), (MB * D // 2) ** -0.5, 0.0546875, ((0, 8), (1, 4))),
        "up_b": noise(splits[7], (D, SB, D), D ** -0.5, 0.25, ((0, 8), (2, 4))),
        "merge_w": noise(splits[8], (2 * D, D), (2 * D) ** -0.5, 0.1875, ((0, 8), (1, 4))),
        "ff_in": noise(splits[9], (D, FF), D ** -0.5, 0.25, ((1, 4),)),
        "ff_out": noise(splits[10], (FF, D), FF ** -0.5, 0.125, ((0, 4),)),
        "norm_gain": jnp.clip(1.0 + 0.18 * jax.random.normal(splits[11], (D,), jnp.float32), 0.1, 1.9),
        "norm_bias": noise(splits[12], (D,), 0.3, 4.0, ((0, 4),), jnp.float32),
        "first_gain": jnp.clip(1.0 + 0.18 * jax.random.normal(splits[13], (D,), jnp.float32), 0.1, 1.9),
        "first_bias": noise(splits[14], (D,), 0.3, 4.0, ((0, 4),), jnp.float32),
        "last_gain": jnp.clip(1.0 + 0.18 * jax.random.normal(splits[15], (D,), jnp.float32), 0.1, 1.9),
        "last_bias": noise(splits[16], (D,), 0.3, 4.0, ((0, 4),), jnp.float32),
        "cotangent": noise(splits[17], (SERIES * L, D), 1.0, 6.0, ((0, 8), (1, 4))),
    }


EPS = 1e-05

@jax.custom_vjp
def low(v):
    return lax.optimization_barrier(v.astype(jnp.bfloat16)).astype(jnp.float32)

@jax.custom_vjp
def low_back(v):
    return v

def low_keep(v):
    return (low(v), None)

def low_pass(kept, grad):
    return (grad,)

def back_keep(v):
    return (v, None)

def back_low(kept, grad):
    return (low(grad),)
low.defvjp(low_keep, low_pass)
low_back.defvjp(back_keep, back_low)

def product(left, right):
    return jnp.dot(left, right, precision=lax.Precision.HIGHEST, preferred_element_type=jnp.float32)

def layer_norm(operand, gain_vec, bias_vec):
    row_mean = lax.optimization_barrier(jnp.mean(operand, axis=-1, keepdims=True))
    row_square = lax.optimization_barrier(jnp.mean(operand * operand, axis=-1, keepdims=True))
    inv_std = lax.rsqrt(row_square - row_mean * row_mean + EPS)
    return (operand - row_mean) * inv_std * gain_vec + bias_vec

def unfold(sequence, span_len):
    padded = jnp.pad(sequence, ((0, 0), (span_len - 1, 0), (0, 0)))
    return jnp.concatenate([padded[:, offset:offset + span_len, :] for offset in range(span_len)], axis=2)

def scale_branch(flat_rows, series_count, down_w, iso_w, up_w, stride, span_len, gain_vec, bias_vec):
    short_rows = series_count * span_len
    down_act = low(jnp.tanh(low_back(product(flat_rows.reshape(short_rows, stride * D), down_w))))
    windows = unfold(down_act.reshape(series_count, span_len, D), span_len).reshape(short_rows, span_len * D)
    iso_act = jnp.tanh(low_back(product(windows, iso_w)))
    middle = low(layer_norm(iso_act + down_act, gain_vec, bias_vec))
    upsampled = low_back(product(middle, up_w.reshape(D, stride * D)).reshape(series_count * L, D))
    return low(layer_norm(jnp.tanh(upsampled) + flat_rows, gain_vec, bias_vec))

def layer_forward(series_in, out_mask, params):
    down_a, iso_a, up_a, down_b, iso_b, up_b, merge_w, ff_in, ff_out, norm_gain, norm_bias, first_gain, first_bias, last_gain, last_bias = params
    series_count = series_in.shape[0]
    flat_rows = series_in.reshape(series_count * L, D)
    branch_a = scale_branch(flat_rows, series_count, down_a, iso_a, up_a, SA, MA, norm_gain, norm_bias)
    branch_b = scale_branch(flat_rows, series_count, down_b, iso_b, up_b, SB, MB, norm_gain, norm_bias)
    merged = low_back(product(jnp.concatenate([branch_a, branch_b], axis=1), merge_w))
    first_out = low(layer_norm(merged, first_gain, first_bias))
    hidden = low(jax.nn.gelu(low_back(product(first_out, ff_in)), approximate=False))
    feed = low_back(product(hidden, ff_out))
    return layer_norm(merged + feed, last_gain, last_bias) * out_mask

def reference(signal, horizon, down_a, iso_a, up_a, down_b, iso_b, up_b, merge_w, ff_in, ff_out, norm_gain, norm_bias, first_gain, first_bias, last_gain, last_bias, cotangent):
    series_group = 4
    params = tuple((item.astype(jnp.float32) for item in (down_a, iso_a, up_a, down_b, iso_b, up_b, merge_w, ff_in, ff_out, norm_gain, norm_bias, first_gain, first_bias, last_gain, last_bias)))
    group_count = SERIES // series_group
    inputs = signal.astype(jnp.float32).reshape(group_count, series_group, L, D)
    lengths = horizon.reshape(group_count, series_group)
    upstream = cotangent.astype(jnp.float32).reshape(group_count, series_group * L, D)
    steps_iota = jnp.arange(L, dtype=jnp.int32)

    def one_group(carry, item):
        group_in, group_len, group_cot = item
        out_mask = (steps_iota[None, :] < IN_LEN + group_len[:, None]).astype(jnp.float32).reshape(series_group * L, 1)
        result, back = jax.vjp(lambda series_in, weights: layer_forward(series_in, out_mask, weights), group_in, params)
        grad_in, grad_params = back(group_cot)
        return (jax.tree.map(jnp.add, carry, grad_params), (result, grad_in))
    start_carry = tuple((jnp.zeros_like(item) for item in params))
    totals, (results, grads_in) = lax.scan(one_group, start_carry, (inputs, lengths, upstream))
    series_out = results.reshape(SERIES * L, D).astype(jnp.bfloat16)
    grad_input = grads_in.reshape(SERIES * L, D)
    return (series_out, grad_input, totals[0], totals[1], totals[2], totals[3], totals[4], totals[5], totals[6], totals[7], totals[8], totals[9], totals[10], totals[11], totals[12], totals[13], totals[14])
```

```python
from functools import partial

import jax
import jax.numpy as jnp
from jax import lax
from jax.sharding import PartitionSpec as P

D = 512
SA = 12
SB = 16
IN_LEN = 96
L = 816
MA = 68
MB = 51


EPS = 1e-05
BF = jnp.bfloat16
F32 = jnp.float32


def matmul(left, right):
    return jnp.dot(left, right, preferred_element_type=F32)


def over_rows(left, right):
    return lax.dot_general(left, right, (((0,), (0,)), ((), ())), preferred_element_type=F32)


def against(left, right):
    return lax.dot_general(left, right, (((1,), (1,)), ((), ())), preferred_element_type=F32)


def swap(value, mask):
    return lax.ppermute(value, "tensor", [(i, i ^ mask) for i in range(4)])


def by_xor(blocks):
    t = lax.axis_index("tensor")
    low = (t % 2) == 0
    high = (t // 2) == 0
    mid = [jnp.where(low, blocks[k], blocks[k ^ 1]) for k in range(4)]
    return [jnp.where(high, mid[k], mid[k ^ 2]) for k in range(4)]


def lanes(value):
    width = value.shape[1] // 4
    return [value[:, i * width : (i + 1) * width] for i in range(4)]


def own_lanes(value):
    width = value.shape[1] // 4
    return lax.dynamic_slice_in_dim(value, lax.axis_index("tensor") * width, width, 1)


def gather_blocks(value):
    across = swap(value, 2)
    return by_xor([value, swap(value, 1), across, swap(across, 1)])


def channel_gather(value):
    return jnp.concatenate(gather_blocks(value), axis=1)


def to_rows(value):
    t = lax.axis_index("tensor")
    count = value.shape[0] // 4
    send = [lax.dynamic_slice_in_dim(value, (t ^ k) * count, count, 0) for k in range(4)]
    return jnp.concatenate(by_xor([send[0]] + [swap(send[k], k) for k in (1, 2, 3)]), axis=1)


def to_channels(value):
    send = by_xor(lanes(value))
    return jnp.concatenate(by_xor([send[0]] + [swap(send[k], k) for k in (1, 2, 3)]), axis=0)


def quarter_sum(blocks):
    send = by_xor(blocks)
    mine = send[0] + swap(send[1].astype(BF), 1).astype(F32)
    other = send[2] + swap(send[3].astype(BF), 1).astype(F32)
    return mine + swap(other.astype(BF), 2).astype(F32)


def ring_order(count):
    return list(range(0, count, 2)) + list(range(1, count, 2))[::-1]


def ring_gather(value):
    count = lax.axis_size("dp")
    order = ring_order(count)
    table = jnp.array(order, jnp.int32)
    place = jnp.array([order.index(i) for i in range(count)], jnp.int32)[lax.axis_index("dp")]
    up = [(order[i], order[(i + 1) % count]) for i in range(count)]
    down = [(b, a) for a, b in up]
    result = jnp.zeros((count,) + value.shape, value.dtype)
    result = lax.dynamic_update_index_in_dim(result, value, lax.axis_index("dp"), 0)
    ahead = behind = value
    for step in range(1, count // 2 + 1):
        ahead = lax.ppermute(ahead, "dp", up)
        result = lax.dynamic_update_index_in_dim(result, ahead, table[(place - step) % count], 0)
        if step <= (count - 1) // 2:
            behind = lax.ppermute(behind, "dp", down)
            result = lax.dynamic_update_index_in_dim(
                result, behind, table[(place + step) % count], 0
            )
    return result


def exchange_sum(blocks):
    got = lax.all_to_all(blocks.astype(BF), "dp", 0, 0, tiled=True)
    return jnp.sum(got.astype(F32), axis=0)


def scatter_sum(value):
    return lax.psum_scatter(value.astype(BF), "dp", scatter_dimension=0, tiled=True).astype(F32)


def norm_forward(operand, gain_vec, bias_vec):
    row_mean = jnp.mean(operand, axis=1, keepdims=True)
    row_square = jnp.mean(operand * operand, axis=1, keepdims=True)
    inv_std = lax.rsqrt(row_square - row_mean * row_mean + EPS)
    normed = (operand - row_mean) * inv_std
    return (normed * gain_vec + bias_vec, (normed, inv_std))


def norm_backward(upstream, gain_vec, stored):
    normed, inv_std = stored
    scaled = upstream * gain_vec
    first_mean = jnp.mean(scaled, axis=1, keepdims=True)
    second_mean = jnp.mean(scaled * normed, axis=1, keepdims=True)
    result = inv_std * (scaled - first_mean - normed * second_mean)
    return (result, jnp.sum(upstream * normed, axis=0), jnp.sum(upstream, axis=0))


def tap_plan(rows_held):
    count = lax.axis_size("dp")
    taps = max(-(-(i * rows_held % D + rows_held) // D) for i in range(count))
    start = lax.axis_index("dp") * rows_held
    return taps, start // D, start % D


def iso_forward(act_all, weight, span_len):
    groups = act_all.shape[0]
    series = act_all.shape[1] // span_len
    taps, first, offset = tap_plan(weight.shape[0])
    wide = lax.dynamic_update_slice_in_dim(
        jnp.zeros((taps * D, weight.shape[1]), BF), weight, offset, 0
    )
    timed = act_all.reshape(groups, series, span_len, D).transpose(2, 0, 1, 3)
    timed = timed.reshape(span_len, groups * series, D)
    timed = jnp.pad(timed, ((span_len - 1, taps), (0, 0), (0, 0)))
    timed = lax.dynamic_slice_in_dim(timed, first, span_len + taps - 1, 0)
    columns = jnp.concatenate([timed[j : j + span_len] for j in range(taps)], axis=2)
    columns = columns.reshape(span_len * groups * series, taps * D)
    pre = matmul(columns, wide).reshape(span_len, groups, series, -1)
    pre = pre.transpose(1, 2, 0, 3).reshape(groups, series * span_len, -1)
    return pre, (columns, wide)


def iso_backward(grad_all, stored, rows_held, span_len):
    columns, wide = stored
    groups = grad_all.shape[0]
    series = grad_all.shape[1] // span_len
    taps, first, offset = tap_plan(rows_held)
    timed = grad_all.reshape(groups, series, span_len, -1).transpose(2, 0, 1, 3)
    timed = timed.reshape(span_len * groups * series, -1)
    grad_wide = over_rows(columns, timed)
    grad_weight = lax.dynamic_slice_in_dim(grad_wide, offset, rows_held, 0)
    spread = against(timed, wide).reshape(span_len, groups * series, taps * D)
    total = jnp.zeros((span_len + taps - 1, groups * series, D), F32)
    for j in range(taps):
        total = total.at[j : j + span_len].add(spread[:, :, j * D : (j + 1) * D])
    padded = jnp.zeros((2 * span_len - 1 + taps, groups * series, D), F32)
    padded = lax.dynamic_update_slice_in_dim(padded, total, first, 0)
    back = padded[span_len - 1 : 2 * span_len - 1].reshape(span_len, groups, series, D)
    return grad_weight, back.transpose(1, 2, 0, 3).reshape(groups, series * span_len, D)


def body(
    signal,
    horizon,
    down_a,
    iso_a,
    up_a,
    down_b,
    iso_b,
    up_b,
    merge_w,
    ff_in,
    ff_out,
    norm_gain,
    norm_bias,
    first_gain,
    first_bias,
    last_gain,
    last_bias,
    cotangent,
):
    row_count, col_count = signal.shape
    part_rows = row_count // 4
    series_count = row_count // L
    short_a = row_count // SA
    short_b = row_count // SB
    t = lax.axis_index("tensor")
    wd_a = ring_gather(down_a).reshape(SA * D, col_count)
    wd_b = ring_gather(down_b).reshape(SB * D, col_count)
    x_full = channel_gather(signal)
    vectors = channel_gather(
        jnp.stack([norm_gain, norm_bias, first_gain, first_bias, last_gain, last_bias])
    )
    n_gain, n_bias, f_gain, f_bias, l_gain, l_bias = (vectors[i : i + 1] for i in range(6))
    cot_rows = to_rows(cotangent)
    wu_a = lax.all_gather(up_a, "dp", axis=0, tiled=True).reshape(D, SA * col_count)
    wu_b = lax.all_gather(up_b, "dp", axis=0, tiled=True).reshape(D, SB * col_count)
    w_merge = channel_gather(ring_gather(merge_w).reshape(2 * D, col_count))
    w_in = channel_gather(ff_in)
    w_out = jnp.concatenate(gather_blocks(ff_out), axis=0)

    window_a = x_full.reshape(short_a, SA * D)
    window_b = x_full.reshape(short_b, SB * D)
    down_act = jnp.concatenate(
        [jnp.tanh(matmul(window_a, wd_a)), jnp.tanh(matmul(window_b, wd_b))], axis=0
    )
    down_low = down_act.astype(BF)
    high = (t // 2) == 0
    low = (t % 2) == 0
    across = swap(down_low, 2)
    pair = jnp.concatenate(
        [jnp.where(high, down_low, across), jnp.where(high, across, down_low)], axis=1
    )
    pair_all = ring_gather(pair)
    mate_all = swap(pair_all, 1)
    even = jnp.where(low, pair_all, mate_all)
    odd = jnp.where(low, mate_all, pair_all)
    down_all = jnp.concatenate(
        [even[..., :col_count], odd[..., :col_count], even[..., col_count:], odd[..., col_count:]],
        axis=2,
    )
    down_full = lax.dynamic_index_in_dim(down_all, lax.axis_index("dp"), 0, keepdims=False)

    part_a, iso_store_a = iso_forward(down_all[:, :short_a], iso_a, MA)
    part_b, iso_store_b = iso_forward(down_all[:, short_a:], iso_b, MB)
    iso_pre = exchange_sum(jnp.concatenate([part_a, part_b], axis=1))
    iso_act = jnp.tanh(channel_gather(iso_pre))
    middle, store_mid = norm_forward(iso_act + down_full.astype(F32), n_gain, n_bias)
    middle = middle.astype(BF)

    up_act_a = jnp.tanh(matmul(middle[:short_a], wu_a).reshape(row_count, col_count))
    up_act_b = jnp.tanh(matmul(middle[short_a:], wu_b).reshape(row_count, col_count))

    x_rows = lax.dynamic_slice_in_dim(x_full, t * part_rows, part_rows, 0).astype(F32)
    branch_a, store_br_a = norm_forward(
        to_rows(up_act_a.astype(BF)).astype(F32) + x_rows, n_gain, n_bias
    )
    branch_b, store_br_b = norm_forward(
        to_rows(up_act_b.astype(BF)).astype(F32) + x_rows, n_gain, n_bias
    )
    merge_in = jnp.concatenate([branch_a.astype(BF), branch_b.astype(BF)], axis=1)
    merged = matmul(merge_in, w_merge)
    first_out, store_first = norm_forward(merged, f_gain, f_bias)
    first_low = first_out.astype(BF)
    hidden_pre = matmul(first_low, w_in)
    hidden = jax.nn.gelu(hidden_pre, approximate=False).astype(BF)
    feed = matmul(hidden, w_out)
    last_out, store_last = norm_forward(merged + feed, l_gain, l_bias)
    position = t * part_rows + lax.broadcasted_iota(jnp.int32, (part_rows, 1), 0)
    limit = jnp.broadcast_to(horizon[:, None], (series_count, L)).reshape(row_count, 1)
    limit = lax.dynamic_slice_in_dim(limit, t * part_rows, part_rows, 0)
    out_mask = (position % L < IN_LEN + limit).astype(F32)
    series_out = to_channels((last_out * out_mask).astype(BF))
    upstream = cot_rows.astype(F32) * out_mask
    grad_sum, grad_last_gain, grad_last_bias = norm_backward(upstream, l_gain, store_last)
    grad_feed = grad_sum.astype(BF)
    grad_ff_out = over_rows(hidden, grad_feed)
    grad_hidden = against(grad_feed, w_out)
    _, gelu_back = jax.vjp(partial(jax.nn.gelu, approximate=False), hidden_pre)
    grad_hpre = gelu_back(grad_hidden)[0].astype(BF)
    grad_ff_in = over_rows(first_low, grad_hpre)
    grad_first = against(grad_hpre, w_in)
    grad_merged_norm, grad_first_gain, grad_first_bias = norm_backward(
        grad_first, f_gain, store_first
    )
    grad_merged = (grad_merged_norm + grad_sum).astype(BF)
    grad_merge = over_rows(merge_in, grad_merged)
    grad_pair = against(grad_merged, w_merge)
    grad_resid_a, gain_one, bias_one = norm_backward(grad_pair[:, :D], n_gain, store_br_a)
    grad_resid_b, gain_two, bias_two = norm_backward(grad_pair[:, D:], n_gain, store_br_b)

    resid_a = to_channels(grad_resid_a.astype(BF)).astype(F32)
    resid_b = to_channels(grad_resid_b.astype(BF)).astype(F32)
    grad_upre_a = (resid_a * (1.0 - up_act_a * up_act_a)).astype(BF).reshape(short_a, -1)
    grad_upre_b = (resid_b * (1.0 - up_act_b * up_act_b)).astype(BF).reshape(short_b, -1)
    part_mid = jnp.concatenate([against(grad_upre_a, wu_a), against(grad_upre_b, wu_b)], axis=0)
    grad_up_a = over_rows(middle[:short_a], grad_upre_a).reshape(D, SA, col_count)
    grad_up_b = over_rows(middle[short_a:], grad_upre_b).reshape(D, SB, col_count)
    blocks = lanes(part_mid)
    keep = jnp.concatenate([jnp.where(low, blocks[0], blocks[1]), jnp.where(low, blocks[2], blocks[3])], axis=1)
    give = jnp.concatenate([jnp.where(low, blocks[1], blocks[0]), jnp.where(low, blocks[3], blocks[2])], axis=1)
    keep = keep + swap(give, 1)
    keep = keep + swap(keep, 2)
    mate = swap(keep, 1)
    even = jnp.where(low, keep, mate)
    odd = jnp.where(low, mate, keep)
    grad_middle = jnp.concatenate(
        [even[:, :col_count], odd[:, :col_count], even[:, col_count:], odd[:, col_count:]], axis=1
    )
    grad_inner, gain_mid, bias_mid = norm_backward(grad_middle, n_gain, store_mid)
    grad_ipre = own_lanes((grad_inner * (1.0 - iso_act * iso_act)).astype(BF))
    grad_ipre_all = ring_gather(grad_ipre)
    grad_iso_a, back_a = iso_backward(grad_ipre_all[:, :short_a], iso_store_a, iso_a.shape[0], MA)
    grad_iso_b, back_b = iso_backward(grad_ipre_all[:, short_a:], iso_store_b, iso_b.shape[0], MB)
    back = jnp.concatenate([back_a, back_b], axis=1)
    groups = back.shape[0]
    back = quarter_sum([back[..., i * col_count : (i + 1) * col_count] for i in range(4)])
    grad_down = exchange_sum(back)
    grad_dpre = ((grad_down + own_lanes(grad_inner)) * (1.0 - down_act * down_act)).astype(BF)
    grad_dpre_a, grad_dpre_b = grad_dpre[:short_a], grad_dpre[short_a:]
    grad_down_a = over_rows(window_a, grad_dpre_a)
    grad_down_b = over_rows(window_b, grad_dpre_b)
    grad_x = against(grad_dpre_a, wd_a).reshape(row_count, D) + against(
        grad_dpre_b, wd_b
    ).reshape(row_count, D)
    grad_input = quarter_sum(lanes(grad_x)) + resid_a + resid_b

    sum_up_a = scatter_sum(grad_up_a)
    sum_up_b = scatter_sum(grad_up_b)
    sum_down_a = scatter_sum(grad_down_a)
    sum_down_b = scatter_sum(grad_down_b)
    sum_merge = scatter_sum(quarter_sum(lanes(grad_merge)))
    ff_own = jnp.concatenate(
        [
            quarter_sum(lanes(grad_ff_in)),
            quarter_sum([grad_ff_out[i * D : (i + 1) * D] for i in range(4)]),
        ],
        axis=0,
    )
    ff_total = ring_gather(scatter_sum(ff_own).astype(BF)).reshape(2 * D, D).astype(F32)
    sums = jnp.stack(
        [
            gain_one + gain_two + 0.25 * gain_mid,
            bias_one + bias_two + 0.25 * bias_mid,
            grad_first_gain,
            grad_first_bias,
            grad_last_gain,
            grad_last_bias,
        ]
    )
    sums = own_lanes(lax.psum(sums, ("dp", "tensor")))
    return (
        series_out,
        grad_input,
        sum_down_a,
        grad_iso_a,
        sum_up_a,
        sum_down_b,
        grad_iso_b,
        sum_up_b,
        sum_merge,
        ff_total[:D],
        ff_total[D:],
        sums[0],
        sums[1],
        sums[2],
        sums[3],
        sums[4],
        sums[5],
    )


def solution(mesh):
    in_specs = (
        P("dp", "tensor"),
        P("dp"),
        P("dp", "tensor"),
        P("dp", "tensor"),
        P("dp", None, "tensor"),
        P("dp", "tensor"),
        P("dp", "tensor"),
        P("dp", None, "tensor"),
        P("dp", "tensor"),
        P(None, "tensor"),
        P("tensor", None),
        P("tensor"),
        P("tensor"),
        P("tensor"),
        P("tensor"),
        P("tensor"),
        P("tensor"),
        P("dp", "tensor"),
    )
    out_specs = (
        P("dp", "tensor"),
        P("dp", "tensor"),
        P("dp", "tensor"),
        P("dp", "tensor"),
        P("dp", None, "tensor"),
        P("dp", "tensor"),
        P("dp", "tensor"),
        P("dp", None, "tensor"),
        P("dp", "tensor"),
        P(None, "tensor"),
        P("tensor", None),
        P("tensor"),
        P("tensor"),
        P("tensor"),
        P("tensor"),
        P("tensor"),
        P("tensor"),
    )
    return jax.shard_map(body, mesh=mesh, in_specs=in_specs, out_specs=out_specs, check_vma=False)
```

```python
from functools import partial

import jax
import jax.numpy as jnp
from jax import lax
from jax.experimental import pallas as pl
from jax.experimental.pallas import tpu as pltpu
from jax.sharding import PartitionSpec as P

D = 512
SA = 12
SB = 16
IN_LEN = 96
L = 816
MA = 68
MB = 51


EPS = 1e-05
BF = jnp.bfloat16
F32 = jnp.float32


XOR = (0, 2, 1, 3)
PARAMS = pltpu.CompilerParams(vmem_limit_bytes=56 << 20)


def dot(left, right):
    return jnp.dot(left, right, preferred_element_type=F32)


def dot_tn(left, right):
    return lax.dot_general(left, right, (((0,), (0,)), ((), ())), preferred_element_type=F32)


def dot_nt(left, right):
    return lax.dot_general(left, right, (((1,), (1,)), ((), ())), preferred_element_type=F32)


def swap(value, mask):
    return lax.ppermute(value, "tensor", [(i, i ^ mask) for i in range(4)])


def by_xor(blocks):
    t = lax.axis_index("tensor")
    low = (t % 2) == 0
    high = (t // 2) == 0
    mid = [jnp.where(low, blocks[k], blocks[k ^ 1]) for k in range(4)]
    return [jnp.where(high, mid[k], mid[k ^ 2]) for k in range(4)]


def lanes(value):
    width = value.shape[1] // 4
    return [value[:, i * width : (i + 1) * width] for i in range(4)]


def own_lanes(value):
    width = value.shape[1] // 4
    return lax.dynamic_slice_in_dim(value, lax.axis_index("tensor") * width, width, 1)


def lane_at(t, k, width=128):
    return pl.ds(pl.multiple_of((t ^ k) * width, width), width)


def ring_order(count):
    return list(range(0, count, 2)) + list(range(1, count, 2))[::-1]


def ring_gather(value):
    count = lax.axis_size("dp")
    order = ring_order(count)
    table = jnp.array(order, jnp.int32)
    place = jnp.array([order.index(i) for i in range(count)], jnp.int32)[lax.axis_index("dp")]
    up = [(order[i], order[(i + 1) % count]) for i in range(count)]
    down = [(b, a) for a, b in up]
    result = jnp.zeros((count,) + value.shape, value.dtype)
    result = lax.dynamic_update_index_in_dim(result, value, lax.axis_index("dp"), 0)
    ahead = behind = value
    for step in range(1, count // 2 + 1):
        ahead = lax.ppermute(ahead, "dp", up)
        result = lax.dynamic_update_index_in_dim(result, ahead, table[(place - step) % count], 0)
        if step <= (count - 1) // 2:
            behind = lax.ppermute(behind, "dp", down)
            result = lax.dynamic_update_index_in_dim(
                result, behind, table[(place + step) % count], 0
            )
    return result


def ring_list(value):
    count = lax.axis_size("dp")
    order = ring_order(count)
    table = jnp.array(order, jnp.int32)
    place = jnp.array([order.index(i) for i in range(count)], jnp.int32)[lax.axis_index("dp")]
    up = [(order[i], order[(i + 1) % count]) for i in range(count)]
    down = [(b, a) for a, b in up]
    ahead = behind = value
    blocks, steps = [value], [0]
    for step in range(1, count // 2 + 1):
        ahead = lax.ppermute(ahead, "dp", up)
        blocks.append(ahead)
        steps.append(-step)
        if step <= (count - 1) // 2:
            behind = lax.ppermute(behind, "dp", down)
            blocks.append(behind)
            steps.append(step)
    return blocks, table[(place + jnp.array(steps, jnp.int32)) % count]


def four(value):
    across = swap(value, 2)
    return [value, across, swap(value, 1), swap(across, 1)]


def after(values, *events):
    return lax.optimization_barrier(tuple(values) + events)[: len(values)]


def exchange_sum(blocks):
    got = lax.all_to_all(blocks.astype(BF), "dp", 0, 0, tiled=True)
    return jnp.sum(got.astype(F32), axis=0)


def scatter_sum(value):
    return lax.psum_scatter(value.astype(BF), "dp", scatter_dimension=0, tiled=True).astype(F32)


def norm_forward(operand, gain_vec, bias_vec):
    row_mean = jnp.mean(operand, axis=1, keepdims=True)
    row_square = jnp.mean(operand * operand, axis=1, keepdims=True)
    inv_std = lax.rsqrt(row_square - row_mean * row_mean + EPS)
    normed = (operand - row_mean) * inv_std
    return (normed * gain_vec + bias_vec, (normed, inv_std))


def norm_backward(upstream, gain_vec, stored):
    normed, inv_std = stored
    scaled = upstream * gain_vec
    first_mean = jnp.mean(scaled, axis=1, keepdims=True)
    second_mean = jnp.mean(scaled * normed, axis=1, keepdims=True)
    result = inv_std * (scaled - first_mean - normed * second_mean)
    return (result, jnp.sum(upstream * normed, axis=0), jnp.sum(upstream, axis=0))


def tap_plan(rows_held, span_len):
    count = lax.axis_size("dp")
    taps = max(-(-(i * rows_held % D + rows_held) // D) for i in range(count))
    start = lax.axis_index("dp") * rows_held
    first = jnp.minimum(start // D, span_len - taps)
    return taps, start - first * D, span_len - taps - first


def xor_order(blocks):
    moved = by_xor(blocks)
    return [moved[0], moved[2], moved[1], moved[3]]


def natural_order(blocks):
    return by_xor([blocks[0], blocks[2], blocks[1], blocks[3]])


def tap_columns(weight, taps, offset):
    width = weight.shape[1]
    wide = lax.dynamic_update_slice_in_dim(jnp.zeros((taps * D, width), BF), weight, offset, 0)
    wide = wide.reshape(taps, 4, D // 4, width)
    wide = xor_order([wide[:, i] for i in range(4)])
    return jnp.concatenate([jnp.concatenate([b[j] for b in wide], axis=0) for j in range(taps)], axis=1)


def tap_rows(grad, rows_held, offset):
    quarter = D // 4
    blocks = [grad[:, i * quarter : (i + 1) * quarter] for i in range(4)]
    wide = jnp.concatenate(natural_order(blocks), axis=1)
    return lax.dynamic_slice_in_dim(wide.reshape(-1, grad.shape[2]), offset, rows_held, 0)


def step_of(rows, span):
    step = lax.broadcasted_iota(jnp.int32, (rows, 128), 0)
    for at in range(span, rows, span):
        step = step - jnp.where(step >= span, span, 0)
    return step


def iso_forward_kernel(spans, reach_ref, pair_ref, mate_ref, w_a_ref, w_b_ref, out_ref):
    base = 0
    for scale, w_ref in enumerate((w_a_ref, w_b_ref)):
        rows, span = spans[scale]
        step = step_of(rows, span)
        reach = reach_ref[scale]
        width = out_ref.shape[2]
        taps = w_ref.shape[1] // width
        for g in range(out_ref.shape[0]):
            x = jnp.concatenate(
                [pair_ref[g, base : base + rows, :], mate_ref[g, base : base + rows, :]], axis=1
            )
            z = jnp.dot(x, w_ref[...], preferred_element_type=F32)
            total = z[:, :width]
            for j in range(1, taps):
                total = jnp.where(step >= 1, pltpu.roll(total, 1, 0), 0.0)
                total = total + z[:, j * width : (j + 1) * width]
            total = jnp.where(step >= reach, pltpu.roll(total, reach, 0), 0.0)
            out_ref[g, base : base + rows, :] = total.astype(BF)
        base += rows


def iso_backward_kernel(
    spans, reach_ref, grad_ref, pair_ref, mate_ref, w_a_ref, w_b_ref, ga_ref, gb_ref, back_ref, cols_ref
):
    base = 0
    start = pl.program_id(0) == 0
    for scale, (w_ref, gw_ref) in enumerate(((w_a_ref, ga_ref), (w_b_ref, gb_ref))):
        rows, span = spans[scale]
        step = step_of(rows, span)
        reach = reach_ref[scale]
        width = grad_ref.shape[2]
        taps = w_ref.shape[1] // width
        count = grad_ref.shape[0]
        for g in range(count):
            part = grad_ref[g, base : base + rows, :].astype(F32)
            part = jnp.where(step + reach < span, pltpu.roll(part, jnp.where(reach > 0, rows - reach, 0), 0), 0.0)
            for j in range(taps - 1, -1, -1):
                cols_ref[g * rows : (g + 1) * rows, j * width : (j + 1) * width] = part.astype(BF)
                if j:
                    part = jnp.where(step + 1 < span, pltpu.roll(part, rows - 1, 0), 0.0)
            back = lax.dot_general(
                cols_ref[g * rows : (g + 1) * rows, : taps * width],
                w_ref[...],
                (((1,), (1,)), ((), ())),
                preferred_element_type=F32,
            )
            back_ref[g, base : base + rows, :] = back.astype(BF)
        for half, x_ref in enumerate((pair_ref, mate_ref)):
            x = jnp.concatenate([x_ref[g, base : base + rows, :] for g in range(count)], axis=0)
            grad = lax.dot_general(
                x,
                cols_ref[: count * rows, : taps * width],
                (((0,), (0,)), ((), ())),
                preferred_element_type=F32,
            )
            tall = x_ref.shape[2]
            for j in range(taps):
                at = (j, slice(half * tall, (half + 1) * tall))
                new = grad[:, j * width : (j + 1) * width]
                gw_ref[at] = jnp.where(start, new, gw_ref[at] + new)
        base += rows


def iso_forward(reach, pair_all, mate_all, wide_a, wide_b, spans):
    groups, rows, half = pair_all.shape
    width = half // 2
    several = 4
    whole = lambda array: pl.BlockSpec(array.shape, lambda i: (0,) * len(array.shape))
    block = lambda width: pl.BlockSpec((several, rows, width), lambda i: (i, 0, 0))
    flops = 2 * groups * sum(r * D * w.shape[1] for (r, _), w in zip(spans, (wide_a, wide_b)))
    return pl.pallas_call(
        partial(iso_forward_kernel, spans),
        grid=(groups // several,),
        in_specs=[
            pl.BlockSpec(memory_space=pltpu.SMEM),
            block(half),
            block(half),
            whole(wide_a),
            whole(wide_b),
        ],
        out_specs=block(width),
        out_shape=jax.ShapeDtypeStruct((groups, rows, width), BF),
        compiler_params=pltpu.CompilerParams(vmem_limit_bytes=50 << 20),
        cost_estimate=pl.CostEstimate(
            flops=flops, bytes_accessed=2 * groups * rows * (D + width), transcendentals=0
        ),
    )(reach, pair_all, mate_all, wide_a, wide_b)


def iso_backward(reach, grad_all, pair_all, mate_all, wide_a, wide_b, spans):
    groups, rows, half = pair_all.shape
    width = half // 2
    several = 4
    whole = lambda array: pl.BlockSpec(array.shape, lambda i: (0,) * len(array.shape))
    block = lambda width: pl.BlockSpec((several, rows, width), lambda i: (i, 0, 0))
    taps = [w.shape[1] // width for w in (wide_a, wide_b)]
    grads = [jax.ShapeDtypeStruct((n, D, width), F32) for n in taps]
    flops = 4 * groups * sum(r * D * w.shape[1] for (r, _), w in zip(spans, (wide_a, wide_b)))
    return pl.pallas_call(
        partial(iso_backward_kernel, spans),
        grid=(groups // several,),
        in_specs=[
            pl.BlockSpec(memory_space=pltpu.SMEM),
            block(width),
            block(half),
            block(half),
            whole(wide_a),
            whole(wide_b),
        ],
        out_specs=[whole(grads[0]), whole(grads[1]), block(D)],
        out_shape=grads + [jax.ShapeDtypeStruct((groups, rows, D), BF)],
        scratch_shapes=[pltpu.VMEM((several * max(r for r, _ in spans), max(taps) * width), BF)],
        compiler_params=pltpu.CompilerParams(vmem_limit_bytes=50 << 20),
        cost_estimate=pl.CostEstimate(
            flops=flops, bytes_accessed=4 * groups * rows * D, transcendentals=0
        ),
    )(reach, grad_all, pair_all, mate_all, wide_a, wide_b)


def total_over(value, axis, count):
    mask = 1
    while mask < count:
        value = value + lax.ppermute(value, axis, [(i, i ^ mask) for i in range(count)])
        mask *= 2
    return value


def whole(array):
    return pl.BlockSpec(array.shape, lambda *_: (0,) * len(array.shape))


def scalars():
    return pl.BlockSpec(memory_space=pltpu.SMEM)


def cost(flops, *arrays):
    size = sum(a.size * a.dtype.itemsize for a in arrays)
    return pl.CostEstimate(flops=int(flops), bytes_accessed=int(size), transcendentals=0)


def shape_of(*dims, kind=F32):
    return jax.ShapeDtypeStruct(dims, kind)


def assemble(out_ref, index_ref, refs):
    rows = refs[0].shape[0]
    for i, ref in enumerate(refs):
        out_ref[pl.ds(pl.multiple_of(index_ref[i] * rows, rows), rows), :] = ref[...]


def strided(ref, start, count, stride):
    parts = [ref[j, pl.ds(start, count, stride=stride), :] for j in range(ref.shape[0])]
    return jnp.concatenate(parts, axis=1).astype(BF)


def positions(rows_held, stride, count):
    taps = max(-(-(i * rows_held % D + rows_held) // D) for i in range(count))
    return taps, [min(i * rows_held // D, stride - taps) for i in range(count)]


def down_kernel(count, place_ref, index_ref, *refs):
    blocks, parts, refs = refs[:4], refs[4 : 4 + 2 * count], refs[4 + 2 * count :]
    act_ref, low_ref, full_ref, xa_ref, xb_ref, xs_ref, wa_ref, wb_ref = refs
    t = place_ref[1]
    rows = blocks[0].shape[0]
    for k, part in zip(XOR, blocks):
        value = part[...]
        xs_ref[t ^ k, :rows, :] = value.astype(F32)
        full_ref[:, lane_at(t, k)] = value
    xs_ref[:, rows:, :] = jnp.zeros((4, xs_ref.shape[1] - rows, 128), F32)
    assemble(wa_ref, index_ref, parts[:count])
    assemble(wb_ref, index_ref, [v.at[: wb_ref.shape[0] // count] for v in parts[count:]])
    for stride, weight, out_ref in ((SA, wa_ref, xa_ref), (SB, wb_ref, xb_ref)):
        size = -(-rows // stride // 16) * 16
        taps, starts = positions(weight.shape[0] // count, stride, count)
        for i, start in enumerate(starts):
            for j in range(taps):
                part = xs_ref[t, pl.ds(start + j, size, stride=stride), :]
                out_ref[i, j * size : (j + 1) * size, :] = part.astype(BF)
    base = 0
    for stride, weight in ((SA, wa_ref), (SB, wb_ref)):
        count = -(-rows // stride // 16) * 16
        total = jnp.zeros((count, weight.shape[1]), F32)
        for r in range(stride):
            window = strided(xs_ref, r, count, stride)
            total = total + dot(window, weight[r * D : (r + 1) * D, :])
        total = jnp.tanh(total)
        act_ref[base : base + count, :] = total
        low_ref[base : base + count, :] = total.astype(BF)
        base += count


def down_forward(place, index, blocks, parts, counts, small, tall):
    rows, width = blocks[0].shape
    count = len(parts) // 2
    taps_a, _ = positions(SA * D // count, SA, count)
    taps_b, _ = positions(SB * D // count, SB, count)
    out = [
        shape_of(small, width),
        shape_of(small, width, kind=BF),
        shape_of(rows, D, kind=BF),
        shape_of(count, taps_a * counts[0], width, kind=BF),
        shape_of(count, taps_b * counts[1], width, kind=BF),
    ]
    return pl.pallas_call(
        partial(down_kernel, len(parts) // 2),
        in_specs=[scalars()] * 2 + [whole(v) for v in (*blocks, *parts)],
        out_specs=[whole(v) for v in out],
        out_shape=out,
        scratch_shapes=[
            pltpu.VMEM((4, tall, 128), F32),
            pltpu.VMEM((SA * D, width), BF),
            pltpu.VMEM((SB * D, width), BF),
        ],
        compiler_params=PARAMS,
        cost_estimate=cost(4 * rows * D * width, *blocks, *parts, *out),
    )(place, index, *blocks, *parts)


def up_kernel(
    place_ref, own_ref, across_ref, mate_ref, last_ref, pair_ref, far_ref, vec_ref, w_ref,
    send_ref, ua_ref, ub_ref, mid_ref, normed_ref, inv_ref, act_ref, ups_ref,
):
    t = place_ref[1]
    act = jnp.tanh(
        jnp.concatenate([own_ref[...], across_ref[...], mate_ref[...], last_ref[...]], axis=1)
    )
    down = jnp.concatenate([pair_ref[0], far_ref[0]], axis=1).astype(F32)
    gain = jnp.concatenate([vec_ref[0:1, lane_at(t, k)] for k in XOR], axis=1)
    bias = jnp.concatenate([vec_ref[1:2, lane_at(t, k)] for k in XOR], axis=1)
    middle, (normed, inv_std) = norm_forward(act + down, gain, bias)
    middle = middle.astype(BF)
    for at, k in enumerate(XOR):
        mid_ref[:, lane_at(t, k)] = middle[:, at * 128 : (at + 1) * 128]
    normed_ref[...] = normed
    inv_ref[...] = jnp.broadcast_to(inv_std, inv_ref.shape)
    act_ref[...] = act[:, :128]
    part_rows = send_ref.shape[2]
    base = column = 0
    for scale, (stride, u_ref) in enumerate(((SA, ua_ref), (SB, ub_ref))):
        count = u_ref.shape[0]
        wide = u_ref.shape[1]
        up = jnp.tanh(dot(mid_ref[base : base + count, :], w_ref[:, column : column + wide]))
        u_ref[...] = up
        for r in range(stride):
            ups_ref[pl.ds(r, count, stride=stride), :] = up[:, r * 128 : (r + 1) * 128]
        for j in range(4):
            send_ref[j, scale] = ups_ref[j * part_rows : (j + 1) * part_rows, :].astype(BF)
        base += count
        column += wide


def up_forward(place, blocks, pair_all, far_all, vec, weight, counts, part_rows, tall):
    small, width = blocks[0].shape
    out = [
        shape_of(4, 2, part_rows, width, kind=BF),
        shape_of(counts[0], SA * width),
        shape_of(counts[1], SB * width),
        shape_of(small, D, kind=BF),
        shape_of(small, D),
        shape_of(small, width),
        shape_of(small, width),
    ]
    group = pl.BlockSpec((1,) + pair_all.shape[1:], lambda i, place: (place[0], 0, 0))
    return pl.pallas_call(
        up_kernel,
        grid_spec=pltpu.PrefetchScalarGridSpec(
            num_scalar_prefetch=1,
            grid=(1,),
            in_specs=[whole(v) for v in blocks] + [group, group, whole(vec), whole(weight)],
            out_specs=[whole(v) for v in out],
            scratch_shapes=[pltpu.VMEM((tall, width), F32)],
        ),
        out_shape=out,
        compiler_params=PARAMS,
        cost_estimate=cost(2 * small * D * weight.shape[1] // 2, weight, *out),
    )(place, *blocks, pair_all, far_all, vec, weight)


def rows_kernel(
    place_ref, horizon_ref, up_ref, x_ref, cot_ref, vec_ref, *refs
):
    weights, merges = refs[:4], refs[4:8]
    out_ref, send_ref, keep_ref, give_ref, sums_ref, wm_ref, slope_ref = refs[8:15]
    hid_ref, hpre_ref, first_ref, feed_ref, pair_ref, merged_ref = refs[15:]
    t = place_ref[1]
    step = pl.program_id(0)
    tile = x_ref.shape[0]
    at = pl.ds(pl.multiple_of(step * tile, tile), tile)
    @pl.when(step == 0)
    def _():
        for k, merge in zip(XOR, merges):
            wm_ref[:, lane_at(t, k)] = merge[...]

    vec = [vec_ref[i : i + 1, :] for i in range(6)]
    x = x_ref[...].astype(F32)
    stored = []
    for scale in range(2):
        up = jnp.concatenate([up_ref[j, scale] for j in range(4)], axis=1).astype(F32)
        branch, kept = norm_forward(up + x, vec[0], vec[1])
        stored.append(kept)
        pair_ref[at, scale * D : (scale + 1) * D] = branch.astype(BF)
    merged = dot(pair_ref[at, :], wm_ref[...])
    first, first_kept = norm_forward(merged, vec[2], vec[3])
    first_ref[at, :] = first.astype(BF)
    feed = jnp.zeros((tile, D), F32)
    for k in range(4):
        pre = dot(first_ref[at, :], weights[k][:D, :])
        chance = 0.5 * (1.0 + lax.erf(pre * (0.5**0.5)))
        slope_ref[:, k * D : (k + 1) * D] = chance + pre * (
            jnp.exp(-0.5 * pre * pre) * 0.3989422804014327
        )
        hid_ref[at, k * D : (k + 1) * D] = (pre * chance).astype(BF)
        feed = feed + dot(hid_ref[at, k * D : (k + 1) * D], weights[k][D:, :])
    last, last_kept = norm_forward(merged + feed, vec[4], vec[5])
    time = step * tile + lax.broadcasted_iota(jnp.int32, (tile, 128), 0)
    mask = (time < IN_LEN + horizon_ref[t]).astype(F32)[:, :1]
    last = (last * mask).astype(BF)
    for j in range(4):
        out_ref[j] = last[:, j * 128 : (j + 1) * 128]
    upstream = jnp.concatenate([cot_ref[j] for j in range(4)], axis=1).astype(F32) * mask
    grad_sum, last_gain, last_bias = norm_backward(upstream, vec[4], last_kept)
    feed_ref[at, :] = grad_sum.astype(BF)
    grad_first = jnp.zeros((tile, D), F32)
    for k in range(4):
        grad_hidden = dot_nt(feed_ref[at, :], weights[k][D:, :])
        hpre_ref[at, k * D : (k + 1) * D] = (
            grad_hidden * slope_ref[:, k * D : (k + 1) * D]
        ).astype(BF)
        grad_first = grad_first + dot_nt(hpre_ref[at, k * D : (k + 1) * D], weights[k][:D, :])
    grad_merged, first_gain, first_bias = norm_backward(grad_first, vec[2], first_kept)
    merged_ref[at, :] = (grad_merged + grad_sum).astype(BF)
    gains = jnp.zeros((D,), F32)
    biases = jnp.zeros((D,), F32)
    for scale in range(2):
        grad_branch = dot_nt(merged_ref[at, :], wm_ref[scale * D : (scale + 1) * D, :])
        grad, gain, bias = norm_backward(grad_branch, vec[0], stored[scale])
        gains, biases = gains + gain, biases + bias
        grad = grad.astype(BF)
        for j in range(4):
            send_ref[j, scale] = grad[:, j * 128 : (j + 1) * 128]
    sums = (gains, biases, first_gain, first_bias, last_gain, last_bias)
    sums = jnp.concatenate([v[None, :] for v in sums] + [jnp.zeros((2, D), F32)], axis=0)
    sums_ref[...] = jnp.where(step == 0, sums, sums_ref[...] + sums)

    @pl.when(step == pl.num_programs(0) - 1)
    def _():
        wide = keep_ref.shape[1] // 2
        for i, (k, ref) in enumerate(zip(XOR, (keep_ref, keep_ref, give_ref, give_ref))):
            block = slice(i * D, (i + 1) * D)
            to = i % 2 * wide
            ref[:D, to : to + D] = dot_tn(first_ref[...], hpre_ref[:, block]).astype(BF)
            ref[D:, to : to + D] = dot_tn(hid_ref[:, block], feed_ref[...]).astype(BF)
            ref[:, to + D : to + wide] = dot_tn(
                pair_ref[...], merged_ref[:, lane_at(t, k)]
            ).astype(BF)


def rows_step(place, horizon, up_rows, x_full, cot_rows, vec, weights, merges):
    part_rows, width = cot_rows.shape[1:]
    steps = 3
    tile = part_rows // steps
    tall, wide = weights[0].shape[0], weights[0].shape[1] + width
    out = [
        shape_of(4, part_rows, width, kind=BF),
        shape_of(4, 2, part_rows, width, kind=BF),
        shape_of(tall, 2 * wide, kind=BF),
        shape_of(tall, 2 * wide, kind=BF),
        shape_of(8, D),
    ]
    three = pl.BlockSpec((4, tile, width), lambda i, place: (0, i, 0))
    four = pl.BlockSpec((4, 2, tile, width), lambda i, place: (0, 0, i, 0))
    once = lambda v: pl.BlockSpec(
        v.shape, lambda *_: (0,) * len(v.shape), pipeline_mode=pl.Buffered(1)
    )
    return pl.pallas_call(
        rows_kernel,
        grid_spec=pltpu.PrefetchScalarGridSpec(
            num_scalar_prefetch=1,
            grid=(steps,),
            in_specs=[
                scalars(),
                four,
                pl.BlockSpec((tile, D), lambda i, place: (place[1] * steps + i, 0)),
                three,
                whole(vec),
                *[once(v) for v in weights + merges],
            ],
            out_specs=[three, four, whole(out[2]), whole(out[3]), whole(out[4])],
            scratch_shapes=[
                pltpu.VMEM((2 * D, D), BF),
                pltpu.VMEM((tile, 4 * D), F32),
                pltpu.VMEM((part_rows, 4 * D), BF),
                pltpu.VMEM((part_rows, 4 * D), BF),
                pltpu.VMEM((part_rows, D), BF),
                pltpu.VMEM((part_rows, D), BF),
                pltpu.VMEM((part_rows, 2 * D), BF),
                pltpu.VMEM((part_rows, D), BF),
            ],
        ),
        out_shape=out,
        compiler_params=PARAMS,
        cost_estimate=cost(6 * part_rows * D * 10 * D, *weights, *merges, *out),
    )(place, horizon, up_rows, x_full, cot_rows, vec, *weights, *merges)


def up_back_kernel(
    place_ref, res_ref, ua_ref, ub_ref, mid_ref, w_ref, keep_ref, give_ref, grad_ref, rs_ref, cols_ref, part_ref
):
    t = place_ref[1]
    part_rows = res_ref.shape[2]
    rows = 4 * part_rows
    rs_ref[rows:, :] = jnp.zeros((rs_ref.shape[0] - rows, 128), F32)
    base = column = 0
    for scale, (stride, u_ref) in enumerate(((SA, ua_ref), (SB, ub_ref))):
        count, wide = u_ref.shape
        for j in range(4):
            rs_ref[j * part_rows : (j + 1) * part_rows, :] = res_ref[j, scale].astype(F32)
        for r in range(stride):
            up = u_ref[:, r * 128 : (r + 1) * 128]
            grad = rs_ref[pl.ds(r, count, stride=stride), :] * (1.0 - up * up)
            cols_ref[:count, r * 128 : (r + 1) * 128] = grad.astype(BF)
        grad = cols_ref[:count, :wide]
        part_ref[base : base + count, :] = dot_nt(grad, w_ref[:, column : column + wide])
        grad_ref[:, column : column + wide] = dot_tn(mid_ref[base : base + count, :], grad).astype(BF)
        base += count
        column += wide
    for slot, ref in enumerate((keep_ref, give_ref)):
        for at in range(2):
            ref[:, at * 128 : (at + 1) * 128] = part_ref[:, lane_at(t, XOR[2 * slot + at])]


def up_backward(place, res, ua, ub, mid, weight, tall):
    small = mid.shape[0]
    width = res.shape[3]
    out = [
        shape_of(small, 2 * width),
        shape_of(small, 2 * width),
        shape_of(D, weight.shape[1], kind=BF),
    ]
    return pl.pallas_call(
        up_back_kernel,
        in_specs=[scalars()] + [whole(v) for v in (res, ua, ub, mid, weight)],
        out_specs=[whole(v) for v in out],
        out_shape=out,
        scratch_shapes=[
            pltpu.VMEM((tall, width), F32),
            pltpu.VMEM((max(ua.shape[0], ub.shape[0]), max(ua.shape[1], ub.shape[1])), BF),
            pltpu.VMEM((small, D), F32),
        ],
        compiler_params=PARAMS,
        cost_estimate=cost(4 * small * D * weight.shape[1] // 2, res, ua, ub, mid, weight, *out),
    )(place, res, ua, ub, mid, weight)


def down_weight_kernel(place_ref, grad_ref, *refs):
    t = place_ref[1]
    several = grad_ref.shape[0]

    @pl.when(pl.program_id(0) == 0)
    def _():
        for out_ref in refs[8:]:
            out_ref[...] = jnp.zeros_like(out_ref)

    base = 0
    for blocks, out_ref in ((refs[:4], refs[8]), (refs[4:8], refs[9])):
        taps = out_ref.shape[0] // D
        count = blocks[0].shape[1] // taps
        for g in range(several):
            grad = grad_ref[g, base : base + count, :]
            for j in range(taps):
                at = slice(j * count, (j + 1) * count)
                x = jnp.concatenate([v[g, at, :] for v in blocks], axis=1)
                part = dot_tn(x, grad)
                for i, k in enumerate(XOR):
                    to = pl.ds(pl.multiple_of(j * D + (t ^ k) * 128, 128), 128)
                    out_ref[to, :] = out_ref[to, :] + part[i * 128 : (i + 1) * 128]
        base += count


def down_weight_grad(place, grad_all, blocks_a, blocks_b, counts):
    groups, small, width = grad_all.shape
    several = 4
    out = [
        shape_of(blocks[0].shape[1] // size * D, width)
        for blocks, size in zip((blocks_a, blocks_b), counts)
    ]
    block = lambda v: pl.BlockSpec((several,) + v.shape[1:], lambda i: (i, 0, 0))
    return pl.pallas_call(
        down_weight_kernel,
        grid=(groups // several,),
        in_specs=[scalars()] + [block(v) for v in (grad_all, *blocks_a, *blocks_b)],
        out_specs=[whole(v) for v in out],
        out_shape=out,
        compiler_params=PARAMS,
        cost_estimate=cost(8 * blocks_a[0].size * 4 * width // 2, grad_all, *blocks_a, *blocks_b),
    )(place, grad_all, *blocks_a, *blocks_b)


def down_input_kernel(count, place_ref, index_ref, grad_ref, *refs):
    parts, (keep_ref, give_ref, gx_ref, wa_ref, wb_ref) = refs[: 2 * count], refs[2 * count :]
    t = place_ref[1]
    rows = keep_ref.shape[0]
    assemble(wa_ref, index_ref, parts[:count])
    assemble(wb_ref, index_ref, [v.at[: wb_ref.shape[0] // count] for v in parts[count:]])
    base = 0
    for stride, weight in ((SA, wa_ref), (SB, wb_ref)):
        count = -(-rows // stride // 16) * 16
        grad = grad_ref[base : base + count, :]
        for r in range(stride):
            at = pl.ds(r, count, stride=stride)
            part = dot_nt(grad, weight[r * D : (r + 1) * D, :])
            for j in range(4):
                lane = slice(j * 128, (j + 1) * 128)
                if base:
                    gx_ref[j, at, :] = gx_ref[j, at, :] + part[:, lane]
                else:
                    gx_ref[j, at, :] = part[:, lane]
        base += count
    for slot, ref in enumerate((keep_ref, give_ref)):
        for i in range(2):
            ref[:, i * 128 : (i + 1) * 128] = gx_ref[t ^ XOR[2 * slot + i], :rows, :].astype(BF)


def down_input_grad(place, index, grad, parts, rows, tall):
    width = grad.shape[1]
    out = [shape_of(rows, 2 * width, kind=BF)] * 2
    return pl.pallas_call(
        partial(down_input_kernel, len(parts) // 2),
        in_specs=[scalars()] * 2 + [whole(v) for v in (grad, *parts)],
        out_specs=[whole(v) for v in out],
        out_shape=out,
        scratch_shapes=[
            pltpu.VMEM((4, tall, 128), F32),
            pltpu.VMEM((SA * D, width), BF),
            pltpu.VMEM((SB * D, width), BF),
        ],
        compiler_params=PARAMS,
        cost_estimate=cost(4 * rows * D * width, grad, *parts, *out),
    )(place, index, grad, *parts)


def body(
    signal,
    horizon,
    down_a,
    iso_a,
    up_a,
    down_b,
    iso_b,
    up_b,
    merge_w,
    ff_in,
    ff_out,
    norm_gain,
    norm_bias,
    first_gain,
    first_bias,
    last_gain,
    last_bias,
    cotangent,
):
    row_count, col_count = signal.shape
    part_rows = row_count // 4
    counts = (row_count // SA, -(-row_count // SB // 16) * 16)
    small = counts[0] + counts[1]
    tall = max(counts[0] * SA, counts[1] * SB)
    spans = ((counts[0], MA), (counts[1], MB))
    t = lax.axis_index("tensor")
    group = lax.axis_index("dp")
    place = jnp.stack([group, t]).astype(jnp.int32)

    x_blocks = four(signal)
    parts_a, index = ring_list(down_a)
    parts_b, _ = ring_list(jnp.concatenate([down_b, merge_w], axis=0))
    parts = parts_a + parts_b
    act, low, x_full, x_send_a, x_send_b = down_forward(
        place, index, x_blocks, parts, counts, small, tall
    )

    vec_own = jnp.stack(
        [norm_gain, norm_bias, first_gain, first_bias, last_gain, last_bias, last_bias, last_bias]
    )
    ff_own = jnp.concatenate([ff_in, ff_out], axis=0)
    vec_own, ff_own = after((vec_own, ff_own), x_blocks[1])
    vec = jnp.concatenate(natural_order(four(vec_own)), axis=1)
    ff_blocks = four(ff_own)
    up_held = jnp.concatenate(
        [up_a.reshape(up_a.shape[0], -1), up_b.reshape(up_b.shape[0], -1)], axis=1
    )
    (up_held,) = after((up_held,), *parts)
    w_up = lax.all_gather(up_held, "dp", axis=0, tiled=True)
    (cot_held,) = after((cotangent,), ff_blocks[1])
    cot_rows = lax.all_to_all(
        cot_held.reshape(4, part_rows, col_count), "tensor", 0, 0, tiled=True
    )
    taps_a, offset_a, reach_a = tap_plan(iso_a.shape[0], MA)
    taps_b, offset_b, reach_b = tap_plan(iso_b.shape[0], MB)
    reach = jnp.stack([reach_a, reach_b]).astype(jnp.int32)
    wide_a = tap_columns(iso_a, taps_a, offset_a)
    wide_b = tap_columns(iso_b, taps_b, offset_b)

    pair_all = ring_gather(jnp.concatenate([low, swap(low, 2)], axis=1))
    far_all = swap(pair_all, 1)
    merge_own = jnp.zeros((len(parts_b),) + merge_w.shape, BF)
    for i, part in enumerate(parts_b):
        merge_own = lax.dynamic_update_index_in_dim(
            merge_own, part[down_b.shape[0] :], index[i], 0
        )
    (merge_own,) = after((merge_own.reshape(2 * D, col_count),), pair_all)
    merge_blocks = four(merge_own)
    iso_pre = exchange_sum(iso_forward(reach, pair_all, far_all, wide_a, wide_b, spans))
    send, up_act_a, up_act_b, middle, normed, inv_std, iso_own = up_forward(
        place, four(iso_pre), pair_all, far_all, vec, w_up, counts, part_rows, tall
    )
    (x_send_a,) = after((x_send_a,), iso_pre)
    x_pos_a = lax.all_to_all(x_send_a, "dp", 0, 0, tiled=True)
    up_rows = lax.all_to_all(send, "tensor", 0, 0, tiled=True)
    x_pos_a, x_send_b = after((x_pos_a, x_send_b), up_rows)
    x_pos_a = four(x_pos_a)
    x_pos_b = lax.all_to_all(x_send_b, "dp", 0, 0, tiled=True)
    last, res_send, keep_w, give_w, sums = rows_step(
        place, horizon, up_rows, x_full, cot_rows, vec, ff_blocks, merge_blocks
    )
    res = lax.all_to_all(res_send, "tensor", 0, 0, tiled=True)
    keep_w, give_w = after((keep_w, give_w), res)
    sum_w = (keep_w.astype(F32) + swap(give_w, 1).astype(F32)).astype(BF)
    sum_w = lax.psum_scatter(sum_w, "dp", scatter_dimension=0, tiled=True)

    keep, give, grad_up = up_backward(place, res, up_act_a, up_act_b, middle, w_up, tall)
    sum_up = lax.psum_scatter(grad_up, "dp", scatter_dimension=0, tiled=True)
    keep = keep + swap(give, 1)
    crossed = swap(keep.astype(BF), 2).astype(F32)
    keep = keep + jnp.concatenate([crossed[:, col_count:], crossed[:, :col_count]], axis=1)
    grad_middle = jnp.concatenate([keep, swap(keep, 1)], axis=1)
    last, sums, x_pos_b = after((last, sums, x_pos_b), grad_middle)
    x_pos_b = four(x_pos_b)
    series_out = lax.all_to_all(last, "tensor", 0, 0, tiled=True).reshape(row_count, col_count)
    x_gain = jnp.concatenate(xor_order(lanes(vec[:1])), axis=1)
    grad_inner, gain_mid, bias_mid = norm_backward(grad_middle, x_gain, (normed, inv_std[:, :1]))
    grad_inner = grad_inner[:, :col_count]
    grad_ipre_all = ring_gather((grad_inner * (1.0 - iso_own * iso_own)).astype(BF))
    grad_wide_a, grad_wide_b, back = iso_backward(
        reach, grad_ipre_all, pair_all, far_all, wide_a, wide_b, spans
    )
    half = 2 * col_count
    kept = back[..., :half].astype(F32) + swap(back[..., half:], 1).astype(F32)
    kept = kept[..., :col_count] + swap(kept[..., col_count:].astype(BF), 2).astype(F32)
    grad_down = exchange_sum(kept)
    grad_dpre = ((grad_down + grad_inner) * (1.0 - act * act)).astype(BF)
    keep_x, give_x = down_input_grad(place, index, grad_dpre, parts, row_count, tall)
    grad_dpre_all = ring_gather(grad_dpre)
    grad_pos_a, grad_pos_b = down_weight_grad(place, grad_dpre_all, x_pos_a, x_pos_b, counts)
    count = lax.axis_size("dp")
    sum_down = []
    for grad, held, stride in ((grad_pos_a, down_a, SA), (grad_pos_b, down_b, SB)):
        rows_held = held.shape[0]
        starts = jnp.array(positions(rows_held, stride, count)[1], jnp.int32)
        offset = group * rows_held - starts[group] * D
        sum_down.append(lax.dynamic_slice_in_dim(grad, offset, rows_held, 0))
    sum_down_a, sum_down_b = sum_down
    keep_x = keep_x.astype(F32) + swap(give_x, 1).astype(F32)
    grad_input = keep_x[:, :col_count] + swap(keep_x[:, col_count:].astype(BF), 2).astype(F32)
    res = res.astype(F32)
    grad_input = grad_input + (res[:, 0] + res[:, 1]).reshape(row_count, col_count)

    grad_iso_a = tap_rows(grad_wide_a, iso_a.shape[0], offset_a)
    grad_iso_b = tap_rows(grad_wide_b, iso_b.shape[0], offset_b)
    (sum_w,) = after((sum_w,), back)
    wide = D + col_count
    sum_w = sum_w[:, :wide].astype(F32) + swap(sum_w[:, wide:], 2).astype(F32)
    sum_merge = sum_w[:, D:]
    ff_total = lax.all_gather(sum_w[:, :D].astype(BF), "dp", axis=0, tiled=True)
    sum_up, ff_total = after((sum_up, ff_total), give_x)
    ff_total = ff_total.astype(F32)
    sum_up = sum_up.astype(F32)
    sum_up_a = sum_up[:, : SA * col_count].reshape(up_a.shape)
    sum_up_b = sum_up[:, SA * col_count :].reshape(up_b.shape)
    sums = total_over(sums, "tensor", 4)
    own = jnp.stack([gain_mid[:col_count], bias_mid[:col_count]])
    own = jnp.pad(own, ((0, 6), (0, 0)))
    sums = total_over(own_lanes(sums) + own, "dp", lax.axis_size("dp"))
    return (
        series_out,
        grad_input,
        sum_down_a,
        grad_iso_a,
        sum_up_a,
        sum_down_b,
        grad_iso_b,
        sum_up_b,
        sum_merge,
        ff_total[:D],
        ff_total[D:],
        sums[0],
        sums[1],
        sums[2],
        sums[3],
        sums[4],
        sums[5],
    )


def solution(mesh):
    in_specs = (
        P("dp", "tensor"),
        P("dp"),
        P("dp", "tensor"),
        P("dp", "tensor"),
        P("dp", None, "tensor"),
        P("dp", "tensor"),
        P("dp", "tensor"),
        P("dp", None, "tensor"),
        P("dp", "tensor"),
        P(None, "tensor"),
        P("tensor", None),
        P("tensor"),
        P("tensor"),
        P("tensor"),
        P("tensor"),
        P("tensor"),
        P("tensor"),
        P("dp", "tensor"),
    )
    out_specs = (
        P("dp", "tensor"),
        P("dp", "tensor"),
        P("dp", "tensor"),
        P("dp", "tensor"),
        P("dp", None, "tensor"),
        P("dp", "tensor"),
        P("dp", "tensor"),
        P("dp", None, "tensor"),
        P("dp", "tensor"),
        P(None, "tensor"),
        P("tensor", None),
        P("tensor"),
        P("tensor"),
        P("tensor"),
        P("tensor"),
        P("tensor"),
        P("tensor"),
    )
    return jax.shard_map(body, mesh=mesh, in_specs=in_specs, out_specs=out_specs, check_vma=False)
```

```python
from functools import partial

import jax
import jax.numpy as jnp
import numpy as np
from jax import lax
from jax.experimental import pallas as pl
from jax.experimental.pallas import tpu as pltpu
from jax.sharding import PartitionSpec as P

D = 512
SA = 12
SB = 16
IN_LEN = 96
L = 816
MA = 68
MB = 51


EPS = 1e-05
BF = jnp.bfloat16
F32 = jnp.float32


XOR = (0, 2, 1, 3)
PARAMS = pltpu.CompilerParams(vmem_limit_bytes=56 << 20)


def dot(left, right):
    return jnp.dot(left, right, preferred_element_type=F32)


def dot_tn(left, right):
    return lax.dot_general(left, right, (((0,), (0,)), ((), ())), preferred_element_type=F32)


def dot_nt(left, right):
    return lax.dot_general(left, right, (((1,), (1,)), ((), ())), preferred_element_type=F32)


def swap(value, mask):
    return lax.ppermute(value, "tensor", [(i, i ^ mask) for i in range(4)])


def by_xor(blocks):
    t = lax.axis_index("tensor")
    low = (t % 2) == 0
    high = (t // 2) == 0
    mid = [jnp.where(low, blocks[k], blocks[k ^ 1]) for k in range(4)]
    return [jnp.where(high, mid[k], mid[k ^ 2]) for k in range(4)]


def lanes(value):
    width = value.shape[1] // 4
    return [value[:, i * width : (i + 1) * width] for i in range(4)]


def own_lanes(value):
    width = value.shape[1] // 4
    return lax.dynamic_slice_in_dim(value, lax.axis_index("tensor") * width, width, 1)


def lane_at(t, k, width=128):
    return pl.ds(pl.multiple_of((t ^ k) * width, width), width)


def ring_order(count):
    return list(range(0, count, 2)) + list(range(1, count, 2))[::-1]


def ring_places(count):
    order = ring_order(count)
    steps = [0]
    for step in range(1, count // 2 + 1):
        steps += [-step, step] if step <= (count - 1) // 2 else [-step]
    places = [[order[(order.index(i) + k) % count] for k in steps] for i in range(count)]
    return np.array(places, np.int32)


def own_row(table):
    start = (lax.axis_index("dp"), jnp.int32(0))
    size = (1, table.shape[1])
    return lax.dynamic_slice(jnp.asarray(table), start, size, allow_negative_indices=False)[0]


def rows_from(value, start, count):
    return lax.dynamic_slice_in_dim(value, start, count, 0, allow_negative_indices=False)


def ring_list(value, halves=False, beside=()):
    beside = list(beside)
    held = []
    count = lax.axis_size("dp")
    order = ring_order(count)
    up = [(order[i], order[(i + 1) % count]) for i in range(count)]
    down = [(b, a) for a, b in up]
    ahead = behind = value
    blocks = [value]
    for step in range(1, count // 2 + 1):
        if step > 2 and beside:
            ahead, *moved = together(ahead, *beside.pop(0)(held))
            held += moved
        if step > (count - 1) // 2 and halves:
            half = value.shape[0] // 2
            first = lax.ppermute(ahead[:half], "dp", up)
            second = lax.ppermute(behind[half:], "dp", down)
            blocks.append(jnp.concatenate([first, second], axis=0))
            continue
        ahead = lax.ppermute(ahead, "dp", up)
        blocks.append(ahead)
        if step <= (count - 1) // 2:
            behind = lax.ppermute(behind, "dp", down)
            blocks.append(behind)
    return (blocks, held) if held else blocks


def ring_stack(value):
    blocks = ring_list(value)
    result = jnp.zeros((len(blocks),) + value.shape, value.dtype)
    for i, block in enumerate(blocks):
        result = lax.dynamic_update_slice(result, block[None], (i,) + (0,) * value.ndim)
    return result


def four(value):
    across = swap(value, 2)
    return [value, across, swap(value, 1), swap(across, 1)]


def exchange(blocks):
    return [blocks[0]] + [swap(v, k) for v, k in zip(blocks[1:], XOR[1:])]


def own_sum(blocks):
    far = blocks[1].astype(F32) + swap(blocks[3], 1).astype(F32)
    near = blocks[0].astype(F32) + swap(blocks[2], 1).astype(F32)
    return near + swap(far.astype(BF), 2).astype(F32)


def after(values, *events):
    return lax.optimization_barrier(tuple(values) + events)[: len(values)]


def together(*values):
    return lax.optimization_barrier(values)


def exchange_sum(blocks):
    got = lax.all_to_all(blocks.astype(BF), "dp", 0, 0, tiled=True)
    return jnp.sum(got.astype(F32), axis=0)


def scatter_sum(value):
    return lax.psum_scatter(value.astype(BF), "dp", scatter_dimension=0, tiled=True).astype(F32)


def norm_forward(operand, gain_vec, bias_vec):
    row_mean = jnp.mean(operand, axis=1, keepdims=True)
    row_square = jnp.mean(operand * operand, axis=1, keepdims=True)
    inv_std = lax.rsqrt(row_square - row_mean * row_mean + EPS)
    normed = (operand - row_mean) * inv_std
    return (normed * gain_vec + bias_vec, (normed, inv_std))


def norm_backward(upstream, gain_vec, stored):
    normed, inv_std = stored
    scaled = upstream * gain_vec
    first_mean = jnp.mean(scaled, axis=1, keepdims=True)
    second_mean = jnp.mean(scaled * normed, axis=1, keepdims=True)
    result = inv_std * (scaled - first_mean - normed * second_mean)
    return (result, jnp.sum(upstream * normed, axis=0), jnp.sum(upstream, axis=0))


def tap_plan(rows_held, span_len, count):
    taps = max(-(-(i * rows_held % D + rows_held) // D) for i in range(count))
    first = [min(i * rows_held // D, span_len - taps) for i in range(count)]
    offset = [i * rows_held - f * D for i, f in enumerate(first)]
    return taps, offset, [span_len - taps - f for f in first]


def xor_order(blocks):
    moved = by_xor(blocks)
    return [moved[0], moved[2], moved[1], moved[3]]


def natural_order(blocks):
    return by_xor([blocks[0], blocks[2], blocks[1], blocks[3]])


def taps_kernel(place_ref, plan_ref, iso_a_ref, iso_b_ref, wide_a_ref, wide_b_ref, tall_ref):
    t = place_ref[1]
    for i, (held_ref, wide_ref) in enumerate(((iso_a_ref, wide_a_ref), (iso_b_ref, wide_b_ref))):
        rows = held_ref.shape[0]
        tall_ref[...] = jnp.zeros_like(tall_ref)
        at = pl.ds(pl.multiple_of(plan_ref[2 + i], 8), rows)
        tall_ref[at, :] = held_ref[...].astype(F32)
        for j in range(wide_ref.shape[1] // 128):
            for slot, k in enumerate(XOR):
                at = pl.ds(pl.multiple_of(j * D + (t ^ k) * 128, 128), 128)
                wide_ref[slot * 128 : (slot + 1) * 128, j * 128 : (j + 1) * 128] = tall_ref[
                    at, :
                ].astype(BF)


def tap_columns(place, plan, iso_a, iso_b, taps):
    width = iso_a.shape[1]
    out = [shape_of(D, n * width, kind=BF) for n in taps]
    return pl.pallas_call(
        taps_kernel,
        in_specs=[scalars()] * 2 + [whole(iso_a), whole(iso_b)],
        out_specs=[whole(v) for v in out],
        out_shape=out,
        scratch_shapes=[pltpu.VMEM((max(taps) * D, width), F32)],
        compiler_params=PARAMS,
        cost_estimate=cost(0, iso_a, iso_b, *out),
    )(place, plan, iso_a, iso_b)


def step_of(rows, span):
    step = lax.broadcasted_iota(jnp.int32, (rows, 128), 0)
    for at in range(span, rows, span):
        step = step - jnp.where(step >= span, span, 0)
    return step


def iso_forward_kernel(spans, reach_ref, index_ref, pair_ref, mate_ref, w_a_ref, w_b_ref, out_ref):
    base = 0
    for scale, w_ref in enumerate((w_a_ref, w_b_ref)):
        rows, span = spans[scale]
        step = step_of(rows, span)
        reach = reach_ref[scale]
        width = out_ref.shape[2]
        taps = w_ref.shape[1] // width
        for g in range(pair_ref.shape[0]):
            to = index_ref[pl.program_id(0) * pair_ref.shape[0] + g]
            x = jnp.concatenate(
                [pair_ref[g, base : base + rows, :], mate_ref[g, base : base + rows, :]], axis=1
            )
            z = jnp.dot(x, w_ref[...], preferred_element_type=F32)
            total = z[:, :width]
            for j in range(1, taps):
                total = jnp.where(step >= 1, pltpu.roll(total, 1, 0), 0.0)
                total = total + z[:, j * width : (j + 1) * width]
            total = jnp.where(step >= reach, pltpu.roll(total, reach, 0), 0.0)
            out_ref[to, base : base + rows, :] = total.astype(BF)
        base += rows


def iso_backward_kernel(
    spans, place_ref, plan_ref, index_ref, grad_ref, pair_ref, mate_ref, w_a_ref, w_b_ref, *refs
):
    ga_ref, gb_ref, backs, (cols_ref, sum_a_ref, sum_b_ref) = refs[0], refs[1], refs[2:6], refs[6:]
    t = place_ref[1]
    base = 0
    for scale, (w_ref, gw_ref) in enumerate(((w_a_ref, sum_a_ref), (w_b_ref, sum_b_ref))):
        rows, span = spans[scale]
        step = step_of(rows, span)
        reach = plan_ref[scale]
        width = grad_ref.shape[2]
        taps = w_ref.shape[1] // width
        count = grad_ref.shape[0]
        for g in range(count):
            part = grad_ref[g, base : base + rows, :].astype(F32)
            turn = jnp.where(reach > 0, rows - reach, 0)
            part = jnp.where(step + reach < span, pltpu.roll(part, turn, 0), 0.0)
            for j in range(taps - 1, -1, -1):
                cols_ref[g * rows : (g + 1) * rows, j * width : (j + 1) * width] = part.astype(BF)
                if j:
                    part = jnp.where(step + 1 < span, pltpu.roll(part, rows - 1, 0), 0.0)
            back = dot_nt(cols_ref[g * rows : (g + 1) * rows, : taps * width], w_ref[...])
            back = back.astype(BF)
            to = index_ref[pl.program_id(0) * count + g] if backs[0].shape[0] > 1 else 0
            for i, back_ref in enumerate(backs):
                back_ref[to, base : base + rows, :] = back[:, i * 128 : (i + 1) * 128]
        for half, x_ref in enumerate((pair_ref, mate_ref)):
            x = jnp.concatenate([x_ref[g, base : base + rows, :] for g in range(count)], axis=0)
            grad = dot_tn(x, cols_ref[: count * rows, : taps * width])
            for j in range(taps):
                for i in range(2):
                    k = XOR[2 * half + i]
                    at = pl.ds(pl.multiple_of(j * D + (t ^ k) * 128, 128), 128)
                    new = grad[i * 128 : (i + 1) * 128, j * width : (j + 1) * width]

                    @pl.when(pl.program_id(0) == 0)
                    def _():
                        gw_ref[at, :] = new

                    @pl.when(pl.program_id(0) > 0)
                    def _():
                        gw_ref[at, :] = gw_ref[at, :] + new

        base += rows

    @pl.when(pl.program_id(0) == pl.num_programs(0) - 1)
    def _():
        for i, (out_ref, sum_ref) in enumerate(((ga_ref, sum_a_ref), (gb_ref, sum_b_ref))):
            at = pl.ds(pl.multiple_of(plan_ref[2 + i], 8), out_ref.shape[0])
            out_ref[...] = sum_ref[at, :]


def iso_forward(reach, index, pair_all, mate_all, wide_a, wide_b, spans):
    groups, rows, half = pair_all.shape
    width = half // 2
    several = 4
    whole = lambda array: pl.BlockSpec(array.shape, lambda i: (0,) * len(array.shape))
    block = lambda width: pl.BlockSpec((several, rows, width), lambda i: (i, 0, 0))
    flops = 2 * groups * sum(r * D * w.shape[1] for (r, _), w in zip(spans, (wide_a, wide_b)))
    return pl.pallas_call(
        partial(iso_forward_kernel, spans),
        grid=(groups // several,),
        in_specs=[
            pl.BlockSpec(memory_space=pltpu.SMEM),
            pl.BlockSpec(memory_space=pltpu.SMEM),
            block(half),
            block(half),
            whole(wide_a),
            whole(wide_b),
        ],
        out_specs=pl.BlockSpec((groups, rows, width), lambda i: (0, 0, 0)),
        out_shape=jax.ShapeDtypeStruct((groups, rows, width), BF),
        compiler_params=pltpu.CompilerParams(vmem_limit_bytes=50 << 20),
        cost_estimate=pl.CostEstimate(
            flops=flops, bytes_accessed=2 * groups * rows * (D + width), transcendentals=0
        ),
    )(reach, index, pair_all, mate_all, wide_a, wide_b)


def iso_backward(place, plan, index, grad_all, pair_all, mate_all, wide_a, wide_b, spans, held):
    groups, rows, half = pair_all.shape
    width = half // 2
    several = 4 if groups <= 8 else 1
    block = lambda width: pl.BlockSpec((several, rows, width), lambda i, *_: (i, 0, 0))
    taps = [w.shape[1] // width for w in (wide_a, wide_b)]
    out = [shape_of(n, width) for n in held] + [shape_of(groups, rows, width, kind=BF)] * 4
    flops = 4 * groups * sum(r * D * w.shape[1] for (r, _), w in zip(spans, (wide_a, wide_b)))
    if several > 1:
        back = whole(out[2])
    else:
        back = pl.BlockSpec((1, rows, width), lambda i, place, plan, index: (index[i], 0, 0))
    specs = pltpu.PrefetchScalarGridSpec(
        num_scalar_prefetch=3,
        grid=(groups // several,),
        in_specs=[block(width), block(half), block(half), whole(wide_a), whole(wide_b)],
        out_specs=[whole(out[0]), whole(out[1])] + [back] * 4,
        scratch_shapes=[
            pltpu.VMEM((several * max(r for r, _ in spans), max(taps) * width), BF),
            pltpu.VMEM((taps[0] * D, width), F32),
            pltpu.VMEM((taps[1] * D, width), F32),
        ],
    )
    return pl.pallas_call(
        partial(iso_backward_kernel, spans),
        grid_spec=specs,
        out_shape=out,
        compiler_params=PARAMS,
        cost_estimate=cost(flops, grad_all, pair_all, mate_all, wide_a, wide_b, *out),
    )(place, plan, index, grad_all, pair_all, mate_all, wide_a, wide_b)


def whole(array):
    return pl.BlockSpec(array.shape, lambda *_: (0,) * len(array.shape))


def scalars():
    return pl.BlockSpec(memory_space=pltpu.SMEM)


def cost(flops, *arrays):
    size = sum(a.size * a.dtype.itemsize for a in arrays)
    return pl.CostEstimate(flops=int(flops), bytes_accessed=int(size), transcendentals=0)


def shape_of(*dims, kind=F32):
    return jax.ShapeDtypeStruct(dims, kind)


def assemble(wa_ref, wb_ref, index_ref, refs):
    rows_a, rows_b = wa_ref.shape[0] // len(refs), wb_ref.shape[0] // len(refs)
    for i, ref in enumerate(refs):
        at = pl.ds(pl.multiple_of(index_ref[i] * rows_a, rows_a), rows_a)
        wa_ref[at, :] = ref[:rows_a, :]
        at = pl.ds(pl.multiple_of(index_ref[i] * rows_b, rows_b), rows_b)
        wb_ref[at, :] = ref[rows_a : rows_a + rows_b, :]


def strided(ref, start, count, stride):
    parts = [ref[j, pl.ds(start, count, stride=stride), :] for j in range(ref.shape[0])]
    return jnp.concatenate(parts, axis=1).astype(BF)


def positions(rows_held, stride, count):
    taps = max(-(-(i * rows_held % D + rows_held) // D) for i in range(count))
    return taps, [min(i * rows_held // D, stride - taps) for i in range(count)]


def down_kernel(count, place_ref, index_ref, *refs):
    blocks, parts, refs = refs[:4], refs[4 : 4 + count], refs[4 + count :]
    act_ref, low_ref, full_ref, send_ref, vec_ref, xs_ref, wa_ref, wb_ref = refs
    t = place_ref[1]
    rows = full_ref.shape[0]
    for k, part in zip(XOR, blocks):
        value = part[:rows, :]
        vec = part[rows:, :].astype(F32)
        vec_ref[:, lane_at(t, k)] = vec[:8] + vec[8:16] + vec[16:24]
        xs_ref[t ^ k, :rows, :] = value.astype(F32)
        full_ref[:, lane_at(t, k)] = value
    xs_ref[:, rows:, :] = jnp.zeros((4, xs_ref.shape[1] - rows, 128), F32)
    assemble(wa_ref, wb_ref, index_ref, parts)
    base = 0
    for stride, weight in ((SA, wa_ref), (SB, wb_ref)):
        size = -(-rows // stride // 16) * 16
        taps, starts = positions(weight.shape[0] // count, stride, count)
        for i, start in enumerate(starts):
            for j in range(taps):
                part = xs_ref[t, pl.ds(start + j, size, stride=stride), :]
                send_ref[i, base + j * size : base + (j + 1) * size, :] = part.astype(BF)
        base += taps * size
    base = 0
    for stride, weight in ((SA, wa_ref), (SB, wb_ref)):
        count = -(-rows // stride // 16) * 16
        total = jnp.zeros((count, weight.shape[1]), F32)
        for r in range(stride):
            window = strided(xs_ref, r, count, stride)
            total = total + dot(window, weight[r * D : (r + 1) * D, :])
        total = jnp.tanh(total)
        act_ref[base : base + count, :] = total
        low_ref[base : base + count, :] = total.astype(BF)
        base += count


def down_forward(place, index, blocks, parts, counts, small, tall):
    rows, width = blocks[0].shape
    rows = rows - 32
    count = len(parts)
    taps_a, _ = positions(SA * D // count, SA, count)
    taps_b, _ = positions(SB * D // count, SB, count)
    out = [
        shape_of(small, width),
        shape_of(small, width, kind=BF),
        shape_of(rows, D, kind=BF),
        shape_of(count, taps_a * counts[0] + taps_b * counts[1], width, kind=BF),
        shape_of(8, D),
    ]
    return pl.pallas_call(
        partial(down_kernel, len(parts)),
        in_specs=[scalars()] * 2 + [whole(v) for v in (*blocks, *parts)],
        out_specs=[whole(v) for v in out],
        out_shape=out,
        scratch_shapes=[
            pltpu.VMEM((4, tall, 128), F32),
            pltpu.VMEM((SA * D, width), BF),
            pltpu.VMEM((SB * D, width), BF),
        ],
        compiler_params=PARAMS,
        cost_estimate=cost(4 * rows * D * width, *blocks, *parts, *out),
    )(place, index, *blocks, *parts)


def up_kernel(
    place_ref, own_ref, across_ref, mate_ref, last_ref, pair_ref, far_ref, vec_ref, wa_ref, wb_ref,
    *refs,
):
    sends, (ua_ref, ub_ref, mid_ref, normed_ref, inv_ref, act_ref, ups_ref) = refs[:4], refs[4:]
    t = place_ref[1]
    act = jnp.tanh(
        jnp.concatenate([own_ref[...], across_ref[...], mate_ref[...], last_ref[...]], axis=1)
    )
    down = jnp.concatenate([pair_ref[0], far_ref[0]], axis=1).astype(F32)
    gain = jnp.concatenate([vec_ref[0:1, lane_at(t, k)] for k in XOR], axis=1)
    bias = jnp.concatenate([vec_ref[1:2, lane_at(t, k)] for k in XOR], axis=1)
    middle, (normed, inv_std) = norm_forward(act + down, gain, bias)
    middle = middle.astype(BF)
    for at, k in enumerate(XOR):
        mid_ref[:, lane_at(t, k)] = middle[:, at * 128 : (at + 1) * 128]
    normed_ref[...] = normed
    inv_ref[...] = jnp.broadcast_to(inv_std, inv_ref.shape)
    act_ref[...] = act[:, :128]
    part_rows = sends[0].shape[1]
    base = 0
    for scale, (stride, u_ref, w_ref) in enumerate(((SA, ua_ref, wa_ref), (SB, ub_ref, wb_ref))):
        count = u_ref.shape[0]
        up = jnp.tanh(dot(mid_ref[base : base + count, :], w_ref[...]))
        u_ref[...] = up
        for r in range(stride):
            ups_ref[pl.ds(r, count, stride=stride), :] = up[:, r * 128 : (r + 1) * 128]
        for k, send_ref in zip(XOR, sends):
            at = pl.ds(pl.multiple_of((t ^ k) * part_rows, part_rows), part_rows)
            send_ref[scale] = ups_ref[at, :].astype(BF)
        base += count


def up_forward(place, blocks, pair_all, far_all, vec, weights, counts, part_rows, tall):
    small, width = blocks[0].shape
    out = [
        *[shape_of(2, part_rows, width, kind=BF)] * 4,
        shape_of(counts[0], SA * width),
        shape_of(counts[1], SB * width),
        shape_of(small, D, kind=BF),
        shape_of(small, D),
        shape_of(small, width),
        shape_of(small, width),
    ]
    group = pl.BlockSpec((1,) + pair_all.shape[1:], lambda *_: (0, 0, 0))
    return pl.pallas_call(
        up_kernel,
        grid_spec=pltpu.PrefetchScalarGridSpec(
            num_scalar_prefetch=1,
            grid=(1,),
            in_specs=[whole(v) for v in blocks] + [group, group, whole(vec)]
            + [whole(v) for v in weights],
            out_specs=[whole(v) for v in out],
            scratch_shapes=[pltpu.VMEM((tall, width), F32)],
        ),
        out_shape=out,
        compiler_params=PARAMS,
        cost_estimate=cost(small * D * (SA + SB) * width, *weights, *out),
    )(place, *blocks, pair_all, far_all, vec, *weights)


def rows_kernel(
    place_ref, horizon_ref, index_ref, x_ref, cot_ref, vec_ref, *refs
):
    ups, weights, merges, out_ref, sends = refs[:4], refs[4:8], refs[8:12], refs[12], refs[13:17]
    keep_ref, give_ref, sums_ref, wm_ref, slope_ref, turn_ref = refs[17:23]
    hid_ref, hpre_ref, first_ref, feed_ref, pair_ref, merged_ref = refs[23:]
    t = place_ref[1]
    step = pl.program_id(0)
    tile = x_ref.shape[0]
    at = pl.ds(pl.multiple_of(step * tile, tile), tile)
    @pl.when(step == 0)
    def _():
        for k, merge in zip(XOR, merges):
            count, held = merge.shape[:2]
            for i in range(count):
                rows = pl.ds(pl.multiple_of(index_ref[i] * held, held), held)
                wm_ref[rows, lane_at(t, k)] = merge[i]

    vec = [vec_ref[i : i + 1, :] for i in range(6)]
    x = x_ref[...].astype(F32)
    stored = []
    for scale in range(2):
        for k, up_ref in zip(XOR, ups):
            turn_ref[:, lane_at(t, k)] = up_ref[scale].astype(F32)
        branch, kept = norm_forward(turn_ref[...] + x, vec[0], vec[1])
        stored.append(kept)
        pair_ref[at, scale * D : (scale + 1) * D] = branch.astype(BF)
    merged = dot(pair_ref[at, :], wm_ref[...])
    first, first_kept = norm_forward(merged, vec[2], vec[3])
    first_ref[at, :] = first.astype(BF)
    feed = jnp.zeros((tile, D), F32)
    for k in range(4):
        pre = dot(first_ref[at, :], weights[k][:D, :])
        chance = 0.5 * (1.0 + lax.erf(pre * (0.5**0.5)))
        slope_ref[:, k * D : (k + 1) * D] = chance + pre * (
            jnp.exp(-0.5 * pre * pre) * 0.3989422804014327
        )
        hid_ref[at, k * D : (k + 1) * D] = (pre * chance).astype(BF)
        feed = feed + dot(hid_ref[at, k * D : (k + 1) * D], weights[k][D:, :])
    last, last_kept = norm_forward(merged + feed, vec[4], vec[5])
    time = step * tile + lax.broadcasted_iota(jnp.int32, (tile, 128), 0)
    mask = (time < IN_LEN + horizon_ref[t]).astype(F32)[:, :1]
    last = (last * mask).astype(BF)
    for j in range(4):
        out_ref[j] = last[:, j * 128 : (j + 1) * 128]
    upstream = jnp.concatenate([cot_ref[j] for j in range(4)], axis=1).astype(F32) * mask
    grad_sum, last_gain, last_bias = norm_backward(upstream, vec[4], last_kept)
    feed_ref[at, :] = grad_sum.astype(BF)
    grad_first = jnp.zeros((tile, D), F32)
    for k in range(4):
        grad_hidden = dot_nt(feed_ref[at, :], weights[k][D:, :])
        hpre_ref[at, k * D : (k + 1) * D] = (
            grad_hidden * slope_ref[:, k * D : (k + 1) * D]
        ).astype(BF)
        grad_first = grad_first + dot_nt(hpre_ref[at, k * D : (k + 1) * D], weights[k][:D, :])
    grad_merged, first_gain, first_bias = norm_backward(grad_first, vec[2], first_kept)
    merged_ref[at, :] = (grad_merged + grad_sum).astype(BF)
    gains = jnp.zeros((D,), F32)
    biases = jnp.zeros((D,), F32)
    for scale in range(2):
        grad_branch = dot_nt(merged_ref[at, :], wm_ref[scale * D : (scale + 1) * D, :])
        grad, gain, bias = norm_backward(grad_branch, vec[0], stored[scale])
        gains, biases = gains + gain, biases + bias
        turn_ref[...] = grad
        for k, send_ref in zip(XOR, sends):
            send_ref[scale] = turn_ref[:, lane_at(t, k)].astype(BF)
    sums = (gains, biases, first_gain, first_bias, last_gain, last_bias)
    sums = jnp.concatenate([v[None, :] for v in sums] + [jnp.zeros((2, D), F32)], axis=0)
    sums_ref[...] = jnp.where(step == 0, sums, sums_ref[...] + sums)

    @pl.when(step == pl.num_programs(0) - 1)
    def _():
        wide = keep_ref.shape[1] // 2
        for i, (k, ref) in enumerate(zip(XOR, (keep_ref, keep_ref, give_ref, give_ref))):
            block = slice(i * D, (i + 1) * D)
            to = i % 2 * wide
            ref[:D, to : to + D] = dot_tn(first_ref[...], hpre_ref[:, block]).astype(BF)
            ref[D:, to : to + D] = dot_tn(hid_ref[:, block], feed_ref[...]).astype(BF)
            ref[:, to + D : to + wide] = dot_tn(
                pair_ref[...], merged_ref[:, lane_at(t, k)]
            ).astype(BF)


def rows_step(place, horizon, index, up_rows, x_full, cot_rows, vec, weights, merges):
    part_rows, width = cot_rows.shape[1:]
    steps = 3
    tile = part_rows // steps
    tall, wide = weights[0].shape[0], weights[0].shape[1] + width
    out = [
        shape_of(4, part_rows, width, kind=BF),
        *[shape_of(2, part_rows, width, kind=BF)] * 4,
        shape_of(tall, 2 * wide, kind=BF),
        shape_of(tall, 2 * wide, kind=BF),
        shape_of(8, D),
    ]
    one_way = pl.BlockSpec((4, tile, width), lambda i, place: (0, i, 0))
    two_way = pl.BlockSpec((2, tile, width), lambda i, place: (0, i, 0))
    once = lambda v: pl.BlockSpec(
        v.shape, lambda *_: (0,) * len(v.shape), pipeline_mode=pl.Buffered(1)
    )
    return pl.pallas_call(
        rows_kernel,
        grid_spec=pltpu.PrefetchScalarGridSpec(
            num_scalar_prefetch=1,
            grid=(steps,),
            in_specs=[
                scalars(),
                scalars(),
                pl.BlockSpec((tile, D), lambda i, place: (place[1] * steps + i, 0)),
                one_way,
                whole(vec),
                *[two_way] * 4,
                *[once(v) for v in weights + merges],
            ],
            out_specs=[one_way, *[two_way] * 4, *[whole(v) for v in out[5:]]],
            scratch_shapes=[
                pltpu.VMEM((2 * D, D), BF),
                pltpu.VMEM((tile, 4 * D), F32),
                pltpu.VMEM((tile, D), F32),
                pltpu.VMEM((part_rows, 4 * D), BF),
                pltpu.VMEM((part_rows, 4 * D), BF),
                pltpu.VMEM((part_rows, D), BF),
                pltpu.VMEM((part_rows, D), BF),
                pltpu.VMEM((part_rows, 2 * D), BF),
                pltpu.VMEM((part_rows, D), BF),
            ],
        ),
        out_shape=out,
        compiler_params=PARAMS,
        cost_estimate=cost(6 * part_rows * D * 10 * D, *weights, *merges, *out),
    )(place, horizon, index, x_full, cot_rows, vec, *up_rows, *weights, *merges)


def up_back_kernel(place_ref, *refs):
    held, (ua_ref, ub_ref, mid_ref, wa_ref, wb_ref) = refs[:4], refs[4:9]
    sums_ref, outs = refs[9], refs[10:14]
    grad_ref, kept_ref, rs_ref, cols_ref, part_ref = refs[14:]
    t = place_ref[1]
    part_rows = held[0].shape[1]
    rows = 4 * part_rows
    rs_ref[rows:, :] = jnp.zeros((rs_ref.shape[0] - rows, 128), F32)
    base = column = 0
    for scale, (stride, u_ref, w_ref) in enumerate(((SA, ua_ref, wa_ref), (SB, ub_ref, wb_ref))):
        count, wide = u_ref.shape
        for k, held_ref in zip(XOR, held):
            at = pl.ds(pl.multiple_of((t ^ k) * part_rows, part_rows), part_rows)
            value = held_ref[scale].astype(F32)
            rs_ref[at, :] = value
            kept_ref[at, :] = kept_ref[at, :] + value if scale else value
        for r in range(stride):
            up = u_ref[:, r * 128 : (r + 1) * 128]
            grad = rs_ref[pl.ds(r, count, stride=stride), :] * (1.0 - up * up)
            cols_ref[:count, r * 128 : (r + 1) * 128] = grad.astype(BF)
        grad = cols_ref[:count, :wide]
        part_ref[base : base + count, :] = dot_nt(grad, w_ref[...])
        grad_ref[:, column : column + wide] = dot_tn(mid_ref[base : base + count, :], grad).astype(BF)
        base += count
        column += wide
    part_ref[base:, :] = sums_ref[...]
    for k, out_ref in zip(XOR, outs):
        out_ref[...] = part_ref[:, lane_at(t, k)]


def up_backward(place, res, ua, ub, mid, weights, sums, tall):
    small = mid.shape[0]
    extra = small + sums.shape[0]
    _, part_rows, width = res[0].shape
    out = [
        *[shape_of(extra, width)] * 4,
        shape_of(D, ua.shape[1] + ub.shape[1], kind=BF),
        shape_of(4 * part_rows, width),
    ]
    return pl.pallas_call(
        up_back_kernel,
        in_specs=[scalars()] + [whole(v) for v in (*res, ua, ub, mid, *weights, sums)],
        out_specs=[whole(v) for v in out],
        out_shape=out,
        scratch_shapes=[
            pltpu.VMEM((tall, width), F32),
            pltpu.VMEM((max(ua.shape[0], ub.shape[0]), max(ua.shape[1], ub.shape[1])), BF),
            pltpu.VMEM((extra, D), F32),
        ],
        compiler_params=PARAMS,
        cost_estimate=cost(2 * small * D * out[4].shape[1], *res, ua, ub, mid, *weights, *out),
    )(place, *res, ua, ub, mid, *weights, sums)


def down_weight_kernel(counts, place_ref, plan_ref, index_ref, grad_ref, *refs):
    t = place_ref[1]
    several = grad_ref.shape[0]

    @pl.when(pl.program_id(0) == 0)
    def _():
        for sum_ref in refs[7:9]:
            sum_ref[...] = jnp.zeros_like(sum_ref)

    blocks = refs[:4]
    base = first = 0
    for count, out_ref in zip(counts, refs[7:9]):
        taps = out_ref.shape[0] // D
        for g in range(several):
            grad = grad_ref[g, base : base + count, :]
            for j in range(taps):
                at = slice(first + j * count, first + (j + 1) * count)
                x = jnp.concatenate([v[g, at, :] for v in blocks], axis=1)
                part = dot_tn(x, grad)
                for i, k in enumerate(XOR):
                    to = pl.ds(pl.multiple_of(j * D + (t ^ k) * 128, 128), 128)
                    out_ref[to, :] = out_ref[to, :] + part[i * 128 : (i + 1) * 128]
        base += count
        first += taps * count
    held_ref = refs[-1]
    held_ref[index_ref[pl.program_id(0)]] = grad_ref[0, base:, :].astype(F32)

    @pl.when(pl.program_id(0) == pl.num_programs(0) - 1)
    def _():
        for i in range(2):
            out_ref, sum_ref = refs[4 + i], refs[7 + i]
            at = pl.ds(pl.multiple_of(plan_ref[4 + i], 8), out_ref.shape[0])
            out_ref[...] = sum_ref[at, :]
        total = held_ref[0]
        for i in range(1, held_ref.shape[0]):
            total = total + held_ref[i]
        refs[6][...] = total


def down_weight_grad(place, plan, index, grad_all, blocks, counts, taps, held):
    groups, small, width = grad_all.shape
    sums = [pltpu.VMEM((n * D, width), F32) for n in taps]
    rest = small - sum(counts)
    sums.append(pltpu.VMEM((groups, rest, width), F32))
    out = [shape_of(n, width) for n in held] + [shape_of(rest, width)]
    block = lambda v: pl.BlockSpec((1,) + v.shape[1:], lambda i, place, plan, index: (index[i], 0, 0))
    return pl.pallas_call(
        partial(down_weight_kernel, counts),
        grid_spec=pltpu.PrefetchScalarGridSpec(
            num_scalar_prefetch=3,
            grid=(groups,),
            in_specs=[pl.BlockSpec((1, small, width), lambda i, *_: (i, 0, 0))]
            + [block(v) for v in blocks],
            out_specs=[whole(v) for v in out],
            scratch_shapes=sums,
        ),
        out_shape=out,
        compiler_params=PARAMS,
        cost_estimate=cost(8 * blocks[0].size * 4 * width // 2, grad_all, *blocks),
    )(place, plan, index, grad_all, *blocks)


def down_input_kernel(count, place_ref, index_ref, grad_ref, *refs):
    parts, refs = refs[:count], refs[count:]
    outs, (gx_ref, wa_ref, wb_ref) = refs[:4], refs[4:]
    t = place_ref[1]
    rows = outs[0].shape[0]
    assemble(wa_ref, wb_ref, index_ref, parts)
    base = 0
    for stride, weight in ((SA, wa_ref), (SB, wb_ref)):
        count = -(-rows // stride // 16) * 16
        grad = grad_ref[base : base + count, :]
        for r in range(stride):
            at = pl.ds(r, count, stride=stride)
            part = dot_nt(grad, weight[r * D : (r + 1) * D, :])
            for j in range(4):
                lane = slice(j * 128, (j + 1) * 128)
                if base:
                    gx_ref[j, at, :] = gx_ref[j, at, :] + part[:, lane]
                else:
                    gx_ref[j, at, :] = part[:, lane]
        base += count
    for k, out_ref in zip(XOR, outs):
        out_ref[...] = gx_ref[t ^ k, :rows, :].astype(BF)


def down_input_grad(place, index, grad, parts, rows, tall):
    width = grad.shape[1]
    out = [shape_of(rows, width, kind=BF)] * 4
    return pl.pallas_call(
        partial(down_input_kernel, len(parts)),
        in_specs=[scalars()] * 2 + [whole(v) for v in (grad, *parts)],
        out_specs=[whole(v) for v in out],
        out_shape=out,
        scratch_shapes=[
            pltpu.VMEM((4, tall, 128), F32),
            pltpu.VMEM((SA * D, width), BF),
            pltpu.VMEM((SB * D, width), BF),
        ],
        compiler_params=PARAMS,
        cost_estimate=cost(4 * rows * D * width, grad, *parts, *out),
    )(place, index, grad, *parts)


def body(
    signal,
    horizon,
    down_a,
    iso_a,
    up_a,
    down_b,
    iso_b,
    up_b,
    merge_w,
    ff_in,
    ff_out,
    norm_gain,
    norm_bias,
    first_gain,
    first_bias,
    last_gain,
    last_bias,
    cotangent,
):
    row_count, col_count = signal.shape
    part_rows = row_count // 4
    counts = (row_count // SA, -(-row_count // SB // 16) * 16)
    small = counts[0] + counts[1]
    tall = max(counts[0] * SA, counts[1] * SB)
    spans = ((counts[0], MA), (counts[1], MB))
    t = lax.axis_index("tensor")
    group = lax.axis_index("dp")
    place = jnp.stack([group, t]).astype(jnp.int32)
    count = lax.axis_size("dp")
    index = own_row(ring_places(count))
    taps_a, *taps_plan_a = tap_plan(iso_a.shape[0], MA, count)
    taps_b, *taps_plan_b = tap_plan(iso_b.shape[0], MB, count)
    down_offsets = [
        [i * v.shape[0] - first * D for i, first in enumerate(positions(v.shape[0], stride, count)[1])]
        for v, stride in ((down_a, SA), (down_b, SB))
    ]
    table = [taps_plan_a[1], taps_plan_b[1], taps_plan_a[0], taps_plan_b[0], *down_offsets]
    plan = own_row(np.array(table, np.int32).T)

    vec_own = jnp.stack(
        [norm_gain, norm_bias, first_gain, first_bias, last_gain, last_bias, last_bias, last_bias]
    )
    split = [lax.reduce_precision(vec_own, 8, 7)]
    split.append(lax.reduce_precision(vec_own - split[0], 8, 7))
    split.append(vec_own - split[0] - split[1])
    split.append(jnp.zeros_like(vec_own))
    x_own = jnp.concatenate([signal] + [v.astype(BF) for v in split], axis=0)
    parts, x_blocks = ring_list(
        jnp.concatenate([down_a, down_b, merge_w], axis=0),
        halves=True,
        beside=(
            lambda _: [swap(x_own, 2)],
            lambda held: [swap(x_own, 1), swap(held[0], 1)],
        ),
    )
    x_blocks = [x_own] + x_blocks

    ff_own, x_blocks[1] = together(jnp.concatenate([ff_in, ff_out], axis=0), x_blocks[1])
    ff_blocks = four(ff_own)
    up_held_a, up_held_b, parts[-1] = together(
        up_a.reshape(up_a.shape[0], -1), up_b.reshape(up_b.shape[0], -1), parts[-1]
    )
    w_up_a = lax.all_gather(up_held_a, "dp", axis=0, tiled=True)
    w_up_b = lax.all_gather(up_held_b, "dp", axis=0, tiled=True)
    act, low, x_full, x_send, vec = down_forward(
        place, index, x_blocks, parts, counts, small, tall
    )
    iso_held = after((iso_a, iso_b), low)
    wide_a, wide_b = tap_columns(place, plan, *iso_held, (taps_a, taps_b))

    low_across = swap(low, 2)
    (cot_held,) = after((cotangent,), low_across)
    cot_rows = lax.all_to_all(
        cot_held.reshape(4, part_rows, col_count), "tensor", 0, 0, tiled=True
    )
    pair_all = ring_stack(jnp.concatenate([low, low_across], axis=1))
    (pair_all,) = after((pair_all,), cot_rows, w_up_a, ff_blocks[1])
    far_all = swap(pair_all, 1)
    merge_own = jnp.stack([v[down_a.shape[0] + down_b.shape[0] :] for v in parts])
    (merge_own,) = after((merge_own,), pair_all)
    merge_blocks = four(merge_own)
    iso_part = iso_forward(plan, index, pair_all, far_all, wide_a, wide_b, spans)
    iso_part, w_up_b = together(iso_part, w_up_b)
    iso_pre = exchange_sum(iso_part)
    *send, up_act_a, up_act_b, middle, normed, inv_std, iso_own = up_forward(
        place, four(iso_pre), pair_all, far_all, vec, (w_up_a, w_up_b), counts, part_rows, tall
    )
    (x_send,) = after((x_send,), iso_pre)
    x_pos = lax.all_to_all(x_send, "dp", 0, 0, tiled=True)
    up_rows = exchange(send)
    (x_full,) = after((x_full,), x_pos)
    last, *out = rows_step(
        place, horizon, index, up_rows, x_full, cot_rows, vec, ff_blocks, merge_blocks
    )
    res_send, (keep_w, give_w, sums) = out[:4], out[4:]
    res = exchange(res_send)
    (keep_w,) = after((keep_w,), res_send[1])
    sum_w = (keep_w.astype(F32) + swap(give_w, 1).astype(F32)).astype(BF)
    sum_w = lax.psum_scatter(sum_w, "dp", scatter_dimension=0, tiled=True)

    *mid_parts, grad_up, resid = up_backward(
        place, res, up_act_a, up_act_b, middle, (w_up_a, w_up_b), sums, tall
    )
    sum_up = lax.psum_scatter(grad_up, "dp", scatter_dimension=0, tiled=True)
    near = mid_parts[0] + swap(mid_parts[2], 1)
    far = mid_parts[1] + swap(mid_parts[3], 1)
    crossed = swap(jnp.concatenate([far, near], axis=1).astype(BF), 2).astype(F32)
    keep = jnp.concatenate([near, far], axis=1) + crossed
    grad_middle = jnp.concatenate([keep, swap(keep, 1)], axis=1)
    last, x_pos, grad_middle = together(last, x_pos, grad_middle)
    sums = grad_middle[small:, :col_count]
    grad_middle = grad_middle[:small]
    series_out = lax.all_to_all(last, "tensor", 0, 0, tiled=True)
    x_pos = four(x_pos)
    x_gain = jnp.concatenate(xor_order(lanes(vec[:1])), axis=1)
    grad_inner, gain_mid, bias_mid = norm_backward(grad_middle, x_gain, (normed, inv_std[:, :1]))
    grad_inner = grad_inner[:, :col_count]
    grad_ipre_all = ring_stack((grad_inner * (1.0 - iso_own * iso_own)).astype(BF))
    grad_iso_a, grad_iso_b, *back = iso_backward(
        place, plan, index, grad_ipre_all, pair_all, far_all, wide_a, wide_b, spans,
        (iso_a.shape[0], iso_b.shape[0]),
    )
    series_out, *back = together(series_out, *back)
    series_out = series_out.reshape(row_count, col_count)
    own_back = own_sum(back)
    sum_w, own_back = together(sum_w, own_back)
    wide = D + col_count
    sum_w = sum_w[:, :wide].astype(F32) + swap(sum_w[:, wide:], 2).astype(F32)
    sum_merge = sum_w[:, D:]
    grad_down = exchange_sum(own_back)
    grad_dpre = ((grad_down + grad_inner) * (1.0 - act * act)).astype(BF)
    x_parts = down_input_grad(place, index, grad_dpre, parts, row_count, tall)
    sums = sums + jnp.pad(
        jnp.stack([gain_mid[:col_count], bias_mid[:col_count]]), ((0, 6), (0, 0))
    )
    sums = jnp.pad(sums, ((0, 8), (0, 0))).astype(BF)
    grad_dpre_all = ring_stack(jnp.concatenate([grad_dpre, sums], axis=0))
    ff_total = lax.all_gather(sum_w[:, :D].astype(BF), "dp", axis=0, tiled=True)
    grad_dpre_all, ff_total = together(grad_dpre_all, ff_total)
    sum_down_a, sum_down_b, sums = down_weight_grad(
        place, plan, index, grad_dpre_all, x_pos, counts,
        [positions(v.shape[0], n, count)[0] for v, n in ((down_a, SA), (down_b, SB))],
        (down_a.shape[0], down_b.shape[0]),
    )
    grad_input = own_sum(x_parts) + resid

    ff_total = ff_total.astype(F32)
    sum_up = sum_up.astype(F32)
    sum_up_a = sum_up[:, : SA * col_count].reshape(up_a.shape)
    sum_up_b = sum_up[:, SA * col_count :].reshape(up_b.shape)
    return (
        series_out,
        grad_input,
        sum_down_a,
        grad_iso_a,
        sum_up_a,
        sum_down_b,
        grad_iso_b,
        sum_up_b,
        sum_merge,
        ff_total[:D],
        ff_total[D:],
        sums[0],
        sums[1],
        sums[2],
        sums[3],
        sums[4],
        sums[5],
    )


def solution(mesh):
    in_specs = (
        P("dp", "tensor"),
        P("dp"),
        P("dp", "tensor"),
        P("dp", "tensor"),
        P("dp", None, "tensor"),
        P("dp", "tensor"),
        P("dp", "tensor"),
        P("dp", None, "tensor"),
        P("dp", "tensor"),
        P(None, "tensor"),
        P("tensor", None),
        P("tensor"),
        P("tensor"),
        P("tensor"),
        P("tensor"),
        P("tensor"),
        P("tensor"),
        P("dp", "tensor"),
    )
    out_specs = (
        P("dp", "tensor"),
        P("dp", "tensor"),
        P("dp", "tensor"),
        P("dp", "tensor"),
        P("dp", None, "tensor"),
        P("dp", "tensor"),
        P("dp", "tensor"),
        P("dp", None, "tensor"),
        P("dp", "tensor"),
        P(None, "tensor"),
        P("tensor", None),
        P("tensor"),
        P("tensor"),
        P("tensor"),
        P("tensor"),
        P("tensor"),
        P("tensor"),
    )
    return jax.shard_map(body, mesh=mesh, in_specs=in_specs, out_specs=out_specs, check_vma=False)
```

```python
from functools import partial

import jax
import jax.numpy as jnp
import numpy as np
from jax import lax
from jax.experimental import pallas as pl
from jax.experimental.pallas import tpu as pltpu
from jax.sharding import PartitionSpec as P

D = 512
SA = 12
SB = 16
IN_LEN = 96
L = 816
MA = 68
MB = 51


EPS = 1e-05
BF = jnp.bfloat16
F32 = jnp.float32


XOR = (0, 2, 1, 3)
PARAMS = pltpu.CompilerParams(vmem_limit_bytes=56 << 20)


def dot(left, right):
    return jnp.dot(left, right, preferred_element_type=F32)


def dot_tn(left, right):
    return lax.dot_general(left, right, (((0,), (0,)), ((), ())), preferred_element_type=F32)


def dot_nt(left, right):
    return lax.dot_general(left, right, (((1,), (1,)), ((), ())), preferred_element_type=F32)


def swap(value, mask):
    return lax.ppermute(value, "tensor", [(i, i ^ mask) for i in range(4)])


def by_xor(blocks):
    t = lax.axis_index("tensor")
    low = (t % 2) == 0
    high = (t // 2) == 0
    mid = [jnp.where(low, blocks[k], blocks[k ^ 1]) for k in range(4)]
    return [jnp.where(high, mid[k], mid[k ^ 2]) for k in range(4)]


def lanes(value):
    width = value.shape[1] // 4
    return [value[:, i * width : (i + 1) * width] for i in range(4)]


def own_lanes(value):
    width = value.shape[1] // 4
    return lax.dynamic_slice_in_dim(value, lax.axis_index("tensor") * width, width, 1)


def lane_at(t, k, width=128):
    return pl.ds(pl.multiple_of((t ^ k) * width, width), width)


def ring_order(count):
    return list(range(0, count, 2)) + list(range(1, count, 2))[::-1]


def ring_places(count):
    order = ring_order(count)
    steps = [0]
    for step in range(1, count // 2 + 1):
        steps += [-step, step] if step <= (count - 1) // 2 else [-step]
    places = [[order[(order.index(i) + k) % count] for k in steps] for i in range(count)]
    return np.array(places, np.int32)


def own_row(table):
    start = (lax.axis_index("dp"), jnp.int32(0))
    size = (1, table.shape[1])
    return lax.dynamic_slice(jnp.asarray(table), start, size, allow_negative_indices=False)[0]


def rows_from(value, start, count):
    return lax.dynamic_slice_in_dim(value, start, count, 0, allow_negative_indices=False)


def ring_list(value, halves=False, beside=()):
    beside = list(beside)
    held = []
    count = lax.axis_size("dp")
    order = ring_order(count)
    up = [(order[i], order[(i + 1) % count]) for i in range(count)]
    down = [(b, a) for a, b in up]
    ahead = behind = value
    blocks = [value]
    for step in range(1, count // 2 + 1):
        if step > 2 and beside:
            ahead, *moved = together(ahead, *beside.pop(0)(held))
            held += moved
        if step > (count - 1) // 2 and halves:
            half = value.shape[0] // 2
            first = lax.ppermute(ahead[:half], "dp", up)
            second = lax.ppermute(behind[half:], "dp", down)
            blocks.append(jnp.concatenate([first, second], axis=0))
            continue
        ahead = lax.ppermute(ahead, "dp", up)
        blocks.append(ahead)
        if step <= (count - 1) // 2:
            behind = lax.ppermute(behind, "dp", down)
            blocks.append(behind)
    return (blocks, held) if held else blocks


def ring_stack(value):
    blocks = ring_list(value)
    result = jnp.zeros((len(blocks),) + value.shape, value.dtype)
    for i, block in enumerate(blocks):
        result = lax.dynamic_update_slice(result, block[None], (i,) + (0,) * value.ndim)
    return result


def four(value):
    across = swap(value, 2)
    return [value, across, swap(value, 1), swap(across, 1)]


def exchange(blocks):
    return [blocks[0]] + [swap(v, k) for v, k in zip(blocks[1:], XOR[1:])]


def own_sum(blocks):
    far = blocks[1].astype(F32) + swap(blocks[3], 1).astype(F32)
    near = blocks[0].astype(F32) + swap(blocks[2], 1).astype(F32)
    return near + swap(far.astype(BF), 2).astype(F32)


def after(values, *events):
    return lax.optimization_barrier(tuple(values) + events)[: len(values)]


def together(*values):
    return lax.optimization_barrier(values)


def exchange_sum(blocks):
    got = lax.all_to_all(blocks.astype(BF), "dp", 0, 0, tiled=True)
    return jnp.sum(got.astype(F32), axis=0)


def scatter_sum(value):
    return lax.psum_scatter(value.astype(BF), "dp", scatter_dimension=0, tiled=True).astype(F32)


def norm_forward(operand, gain_vec, bias_vec):
    row_mean = jnp.mean(operand, axis=1, keepdims=True)
    row_square = jnp.mean(operand * operand, axis=1, keepdims=True)
    inv_std = lax.rsqrt(row_square - row_mean * row_mean + EPS)
    normed = (operand - row_mean) * inv_std
    return (normed * gain_vec + bias_vec, (normed, inv_std))


def norm_backward(upstream, gain_vec, stored):
    normed, inv_std = stored
    scaled = upstream * gain_vec
    first_mean = jnp.mean(scaled, axis=1, keepdims=True)
    second_mean = jnp.mean(scaled * normed, axis=1, keepdims=True)
    result = inv_std * (scaled - first_mean - normed * second_mean)
    return (result, jnp.sum(upstream * normed, axis=0), jnp.sum(upstream, axis=0))


def tap_plan(rows_held, span_len, count):
    taps = max(-(-(i * rows_held % D + rows_held) // D) for i in range(count))
    first = [min(i * rows_held // D, span_len - taps) for i in range(count)]
    offset = [i * rows_held - f * D for i, f in enumerate(first)]
    return taps, offset, [span_len - taps - f for f in first]


def xor_order(blocks):
    moved = by_xor(blocks)
    return [moved[0], moved[2], moved[1], moved[3]]


def natural_order(blocks):
    return by_xor([blocks[0], blocks[2], blocks[1], blocks[3]])


def taps_kernel(place_ref, plan_ref, iso_a_ref, iso_b_ref, wide_a_ref, wide_b_ref, tall_ref):
    t = place_ref[1]
    for i, (held_ref, wide_ref) in enumerate(((iso_a_ref, wide_a_ref), (iso_b_ref, wide_b_ref))):
        rows = held_ref.shape[0]
        tall_ref[...] = jnp.zeros_like(tall_ref)
        at = pl.ds(pl.multiple_of(plan_ref[2 + i], 8), rows)
        tall_ref[at, :] = held_ref[...].astype(F32)
        for j in range(wide_ref.shape[1] // 128):
            for slot, k in enumerate(XOR):
                at = pl.ds(pl.multiple_of(j * D + (t ^ k) * 128, 128), 128)
                wide_ref[slot * 128 : (slot + 1) * 128, j * 128 : (j + 1) * 128] = tall_ref[
                    at, :
                ].astype(BF)


def tap_columns(place, plan, iso_a, iso_b, taps):
    width = iso_a.shape[1]
    out = [shape_of(D, n * width, kind=BF) for n in taps]
    return pl.pallas_call(
        taps_kernel,
        in_specs=[scalars()] * 2 + [whole(iso_a), whole(iso_b)],
        out_specs=[whole(v) for v in out],
        out_shape=out,
        scratch_shapes=[pltpu.VMEM((max(taps) * D, width), F32)],
        compiler_params=PARAMS,
        cost_estimate=cost(0, iso_a, iso_b, *out),
    )(place, plan, iso_a, iso_b)


def step_of(rows, span):
    step = lax.broadcasted_iota(jnp.int32, (rows, 128), 0)
    for at in range(span, rows, span):
        step = step - jnp.where(step >= span, span, 0)
    return step


def iso_forward_kernel(spans, reach_ref, index_ref, pair_ref, mate_ref, w_a_ref, w_b_ref, out_ref):
    base = 0
    for scale, w_ref in enumerate((w_a_ref, w_b_ref)):
        rows, span = spans[scale]
        step = step_of(rows, span)
        reach = reach_ref[scale]
        width = out_ref.shape[2]
        taps = w_ref.shape[1] // width
        for g in range(pair_ref.shape[0]):
            to = index_ref[pl.program_id(0) * pair_ref.shape[0] + g]
            x = jnp.concatenate(
                [pair_ref[g, base : base + rows, :], mate_ref[g, base : base + rows, :]], axis=1
            )
            z = jnp.dot(x, w_ref[...], preferred_element_type=F32)
            total = z[:, :width]
            for j in range(1, taps):
                total = jnp.where(step >= 1, pltpu.roll(total, 1, 0), 0.0)
                total = total + z[:, j * width : (j + 1) * width]
            total = jnp.where(step >= reach, pltpu.roll(total, reach, 0), 0.0)
            out_ref[to, base : base + rows, :] = total.astype(BF)
        base += rows


def iso_backward_kernel(
    spans, place_ref, plan_ref, index_ref, grad_ref, pair_ref, mate_ref, w_a_ref, w_b_ref, *refs
):
    ga_ref, gb_ref, backs, (cols_ref, sum_a_ref, sum_b_ref) = refs[0], refs[1], refs[2:6], refs[6:]
    t = place_ref[1]
    base = 0
    for scale, (w_ref, gw_ref) in enumerate(((w_a_ref, sum_a_ref), (w_b_ref, sum_b_ref))):
        rows, span = spans[scale]
        step = step_of(rows, span)
        reach = plan_ref[scale]
        width = grad_ref.shape[2]
        taps = w_ref.shape[1] // width
        count = grad_ref.shape[0]
        for g in range(count):
            part = grad_ref[g, base : base + rows, :].astype(F32)
            turn = jnp.where(reach > 0, rows - reach, 0)
            part = jnp.where(step + reach < span, pltpu.roll(part, turn, 0), 0.0)
            for j in range(taps - 1, -1, -1):
                cols_ref[g * rows : (g + 1) * rows, j * width : (j + 1) * width] = part.astype(BF)
                if j:
                    part = jnp.where(step + 1 < span, pltpu.roll(part, rows - 1, 0), 0.0)
            back = dot_nt(cols_ref[g * rows : (g + 1) * rows, : taps * width], w_ref[...])
            back = back.astype(BF)
            to = index_ref[pl.program_id(0) * count + g] if backs[0].shape[0] > 1 else 0
            for i, back_ref in enumerate(backs):
                back_ref[to, base : base + rows, :] = back[:, i * 128 : (i + 1) * 128]
        for half, x_ref in enumerate((pair_ref, mate_ref)):
            x = jnp.concatenate([x_ref[g, base : base + rows, :] for g in range(count)], axis=0)
            grad = dot_tn(x, cols_ref[: count * rows, : taps * width])
            for j in range(taps):
                for i in range(2):
                    k = XOR[2 * half + i]
                    at = pl.ds(pl.multiple_of(j * D + (t ^ k) * 128, 128), 128)
                    new = grad[i * 128 : (i + 1) * 128, j * width : (j + 1) * width]

                    @pl.when(pl.program_id(0) == 0)
                    def _():
                        gw_ref[at, :] = new

                    @pl.when(pl.program_id(0) > 0)
                    def _():
                        gw_ref[at, :] = gw_ref[at, :] + new

        base += rows

    @pl.when(pl.program_id(0) == pl.num_programs(0) - 1)
    def _():
        for i, (out_ref, sum_ref) in enumerate(((ga_ref, sum_a_ref), (gb_ref, sum_b_ref))):
            at = pl.ds(pl.multiple_of(plan_ref[2 + i], 8), out_ref.shape[0])
            out_ref[...] = sum_ref[at, :]


def iso_forward(reach, index, pair_all, mate_all, wide_a, wide_b, spans):
    groups, rows, half = pair_all.shape
    width = half // 2
    several = 4
    whole = lambda array: pl.BlockSpec(array.shape, lambda i: (0,) * len(array.shape))
    block = lambda width: pl.BlockSpec((several, rows, width), lambda i: (i, 0, 0))
    flops = 2 * groups * sum(r * D * w.shape[1] for (r, _), w in zip(spans, (wide_a, wide_b)))
    return pl.pallas_call(
        partial(iso_forward_kernel, spans),
        grid=(groups // several,),
        in_specs=[
            pl.BlockSpec(memory_space=pltpu.SMEM),
            pl.BlockSpec(memory_space=pltpu.SMEM),
            block(half),
            block(half),
            whole(wide_a),
            whole(wide_b),
        ],
        out_specs=pl.BlockSpec((groups, rows, width), lambda i: (0, 0, 0)),
        out_shape=jax.ShapeDtypeStruct((groups, rows, width), BF),
        compiler_params=pltpu.CompilerParams(vmem_limit_bytes=50 << 20),
        cost_estimate=pl.CostEstimate(
            flops=flops, bytes_accessed=2 * groups * rows * (D + width), transcendentals=0
        ),
    )(reach, index, pair_all, mate_all, wide_a, wide_b)


def iso_backward(place, plan, index, grad_all, pair_all, mate_all, wide_a, wide_b, spans, held):
    groups, rows, half = pair_all.shape
    width = half // 2
    several = 4 if groups <= 8 else 1
    block = lambda width: pl.BlockSpec((several, rows, width), lambda i, *_: (i, 0, 0))
    taps = [w.shape[1] // width for w in (wide_a, wide_b)]
    out = [shape_of(n, width) for n in held] + [shape_of(groups, rows, width, kind=BF)] * 4
    flops = 4 * groups * sum(r * D * w.shape[1] for (r, _), w in zip(spans, (wide_a, wide_b)))
    if several > 1:
        back = whole(out[2])
    else:
        back = pl.BlockSpec((1, rows, width), lambda i, place, plan, index: (index[i], 0, 0))
    specs = pltpu.PrefetchScalarGridSpec(
        num_scalar_prefetch=3,
        grid=(groups // several,),
        in_specs=[block(width), block(half), block(half), whole(wide_a), whole(wide_b)],
        out_specs=[whole(out[0]), whole(out[1])] + [back] * 4,
        scratch_shapes=[
            pltpu.VMEM((several * max(r for r, _ in spans), max(taps) * width), BF),
            pltpu.VMEM((taps[0] * D, width), F32),
            pltpu.VMEM((taps[1] * D, width), F32),
        ],
    )
    return pl.pallas_call(
        partial(iso_backward_kernel, spans),
        grid_spec=specs,
        out_shape=out,
        compiler_params=PARAMS,
        cost_estimate=cost(flops, grad_all, pair_all, mate_all, wide_a, wide_b, *out),
    )(place, plan, index, grad_all, pair_all, mate_all, wide_a, wide_b)


def whole(array):
    return pl.BlockSpec(array.shape, lambda *_: (0,) * len(array.shape))


def scalars():
    return pl.BlockSpec(memory_space=pltpu.SMEM)


def cost(flops, *arrays):
    size = sum(a.size * a.dtype.itemsize for a in arrays)
    return pl.CostEstimate(flops=int(flops), bytes_accessed=int(size), transcendentals=0)


def shape_of(*dims, kind=F32):
    return jax.ShapeDtypeStruct(dims, kind)


def assemble(wa_ref, wb_ref, index_ref, refs):
    rows_a, rows_b = wa_ref.shape[0] // len(refs), wb_ref.shape[0] // len(refs)
    for i, ref in enumerate(refs):
        at = pl.ds(pl.multiple_of(index_ref[i] * rows_a, rows_a), rows_a)
        wa_ref[at, :] = ref[:rows_a, :]
        at = pl.ds(pl.multiple_of(index_ref[i] * rows_b, rows_b), rows_b)
        wb_ref[at, :] = ref[rows_a : rows_a + rows_b, :]


def strided(ref, start, count, stride):
    parts = [ref[j, pl.ds(start, count, stride=stride), :] for j in range(ref.shape[0])]
    return jnp.concatenate(parts, axis=1).astype(BF)


def positions(rows_held, stride, count):
    taps = max(-(-(i * rows_held % D + rows_held) // D) for i in range(count))
    return taps, [min(i * rows_held // D, stride - taps) for i in range(count)]


def down_kernel(count, place_ref, index_ref, *refs):
    blocks, parts, refs = refs[:4], refs[4 : 4 + count], refs[4 + count :]
    act_ref, low_ref, full_ref, send_ref, vec_ref, xs_ref, wa_ref, wb_ref = refs
    t = place_ref[1]
    rows = full_ref.shape[0]
    for k, part in zip(XOR, blocks):
        value = part[:rows, :]
        vec = part[rows:, :].astype(F32)
        vec_ref[:, lane_at(t, k)] = vec[:8] + vec[8:16] + vec[16:24]
        xs_ref[t ^ k, :rows, :] = value.astype(F32)
        full_ref[:, lane_at(t, k)] = value
    xs_ref[:, rows:, :] = jnp.zeros((4, xs_ref.shape[1] - rows, 128), F32)
    assemble(wa_ref, wb_ref, index_ref, parts)
    base = 0
    for stride, weight in ((SA, wa_ref), (SB, wb_ref)):
        size = -(-rows // stride // 16) * 16
        taps, starts = positions(weight.shape[0] // count, stride, count)
        for i, start in enumerate(starts):
            for j in range(taps):
                part = xs_ref[t, pl.ds(start + j, size, stride=stride), :]
                send_ref[i, base + j * size : base + (j + 1) * size, :] = part.astype(BF)
        base += taps * size
    base = 0
    for stride, weight in ((SA, wa_ref), (SB, wb_ref)):
        count = -(-rows // stride // 16) * 16
        total = jnp.zeros((count, weight.shape[1]), F32)
        for r in range(stride):
            window = strided(xs_ref, r, count, stride)
            total = total + dot(window, weight[r * D : (r + 1) * D, :])
        total = jnp.tanh(total)
        act_ref[base : base + count, :] = total
        low_ref[base : base + count, :] = total.astype(BF)
        base += count


def down_forward(place, index, blocks, parts, counts, small, tall):
    rows, width = blocks[0].shape
    rows = rows - 32
    count = len(parts)
    taps_a, _ = positions(SA * D // count, SA, count)
    taps_b, _ = positions(SB * D // count, SB, count)
    out = [
        shape_of(small, width),
        shape_of(small, width, kind=BF),
        shape_of(rows, D, kind=BF),
        shape_of(count, taps_a * counts[0] + taps_b * counts[1], width, kind=BF),
        shape_of(8, D),
    ]
    return pl.pallas_call(
        partial(down_kernel, len(parts)),
        in_specs=[scalars()] * 2 + [whole(v) for v in (*blocks, *parts)],
        out_specs=[whole(v) for v in out],
        out_shape=out,
        scratch_shapes=[
            pltpu.VMEM((4, tall, 128), F32),
            pltpu.VMEM((SA * D, width), BF),
            pltpu.VMEM((SB * D, width), BF),
        ],
        compiler_params=PARAMS,
        cost_estimate=cost(4 * rows * D * width, *blocks, *parts, *out),
    )(place, index, *blocks, *parts)


def up_kernel(
    place_ref, own_ref, across_ref, mate_ref, last_ref, pair_ref, far_ref, vec_ref, wa_ref, wb_ref,
    *refs,
):
    sends, (ua_ref, ub_ref, mid_ref, normed_ref, inv_ref, act_ref, ups_ref) = refs[:4], refs[4:]
    t = place_ref[1]
    act = jnp.tanh(
        jnp.concatenate([own_ref[...], across_ref[...], mate_ref[...], last_ref[...]], axis=1)
    )
    down = jnp.concatenate([pair_ref[0], far_ref[0]], axis=1).astype(F32)
    gain = jnp.concatenate([vec_ref[0:1, lane_at(t, k)] for k in XOR], axis=1)
    bias = jnp.concatenate([vec_ref[1:2, lane_at(t, k)] for k in XOR], axis=1)
    middle, (normed, inv_std) = norm_forward(act + down, gain, bias)
    middle = middle.astype(BF)
    for at, k in enumerate(XOR):
        mid_ref[:, lane_at(t, k)] = middle[:, at * 128 : (at + 1) * 128]
    normed_ref[...] = normed
    inv_ref[...] = jnp.broadcast_to(inv_std, inv_ref.shape)
    act_ref[...] = act[:, :128]
    part_rows = sends[0].shape[1]
    base = 0
    for scale, (stride, u_ref, w_ref) in enumerate(((SA, ua_ref, wa_ref), (SB, ub_ref, wb_ref))):
        count = u_ref.shape[0]
        up = jnp.tanh(dot(mid_ref[base : base + count, :], w_ref[...]))
        u_ref[...] = up
        for r in range(stride):
            ups_ref[pl.ds(r, count, stride=stride), :] = up[:, r * 128 : (r + 1) * 128]
        for k, send_ref in zip(XOR, sends):
            at = pl.ds(pl.multiple_of((t ^ k) * part_rows, part_rows), part_rows)
            send_ref[scale] = ups_ref[at, :].astype(BF)
        base += count


def up_forward(place, blocks, pair_all, far_all, vec, weights, counts, part_rows, tall):
    small, width = blocks[0].shape
    out = [
        *[shape_of(2, part_rows, width, kind=BF)] * 4,
        shape_of(counts[0], SA * width),
        shape_of(counts[1], SB * width),
        shape_of(small, D, kind=BF),
        shape_of(small, D),
        shape_of(small, width),
        shape_of(small, width),
    ]
    group = pl.BlockSpec((1,) + pair_all.shape[1:], lambda *_: (0, 0, 0))
    return pl.pallas_call(
        up_kernel,
        grid_spec=pltpu.PrefetchScalarGridSpec(
            num_scalar_prefetch=1,
            grid=(1,),
            in_specs=[whole(v) for v in blocks] + [group, group, whole(vec)]
            + [whole(v) for v in weights],
            out_specs=[whole(v) for v in out],
            scratch_shapes=[pltpu.VMEM((tall, width), F32)],
        ),
        out_shape=out,
        compiler_params=PARAMS,
        cost_estimate=cost(small * D * (SA + SB) * width, *weights, *out),
    )(place, *blocks, pair_all, far_all, vec, *weights)


def rows_kernel(
    place_ref, horizon_ref, index_ref, x_ref, cot_ref, vec_ref, *refs
):
    ups, weights, merges, out_ref, sends = refs[:4], refs[4:8], refs[8:12], refs[12], refs[13:17]
    keep_ref, give_ref, sums_ref, wm_ref, slope_ref, turn_ref = refs[17:23]
    hid_ref, hpre_ref, first_ref, feed_ref, pair_ref, merged_ref = refs[23:]
    t = place_ref[1]
    step = pl.program_id(0)
    tile = x_ref.shape[0]
    at = pl.ds(pl.multiple_of(step * tile, tile), tile)
    @pl.when(step == 0)
    def _():
        for k, merge in zip(XOR, merges):
            count, held = merge.shape[:2]
            for i in range(count):
                rows = pl.ds(pl.multiple_of(index_ref[i] * held, held), held)
                wm_ref[rows, lane_at(t, k)] = merge[i]

    vec = [vec_ref[i : i + 1, :] for i in range(6)]
    x = x_ref[...].astype(F32)
    stored = []
    for scale in range(2):
        for k, up_ref in zip(XOR, ups):
            turn_ref[:, lane_at(t, k)] = up_ref[scale].astype(F32)
        branch, kept = norm_forward(turn_ref[...] + x, vec[0], vec[1])
        stored.append(kept)
        pair_ref[at, scale * D : (scale + 1) * D] = branch.astype(BF)
    merged = dot(pair_ref[at, :], wm_ref[...])
    first, first_kept = norm_forward(merged, vec[2], vec[3])
    first_ref[at, :] = first.astype(BF)
    feed = jnp.zeros((tile, D), F32)
    for k in range(4):
        pre = dot(first_ref[at, :], weights[k][:D, :])
        chance = 0.5 * (1.0 + lax.erf(pre * (0.5**0.5)))
        slope_ref[:, k * D : (k + 1) * D] = chance + pre * (
            jnp.exp(-0.5 * pre * pre) * 0.3989422804014327
        )
        hid_ref[at, k * D : (k + 1) * D] = (pre * chance).astype(BF)
        feed = feed + dot(hid_ref[at, k * D : (k + 1) * D], weights[k][D:, :])
    last, last_kept = norm_forward(merged + feed, vec[4], vec[5])
    time = step * tile + lax.broadcasted_iota(jnp.int32, (tile, 128), 0)
    mask = (time < IN_LEN + horizon_ref[t]).astype(F32)[:, :1]
    last = (last * mask).astype(BF)
    for j in range(4):
        out_ref[j] = last[:, j * 128 : (j + 1) * 128]
    upstream = jnp.concatenate([cot_ref[j] for j in range(4)], axis=1).astype(F32) * mask
    grad_sum, last_gain, last_bias = norm_backward(upstream, vec[4], last_kept)
    feed_ref[at, :] = grad_sum.astype(BF)
    grad_first = jnp.zeros((tile, D), F32)
    for k in range(4):
        grad_hidden = dot_nt(feed_ref[at, :], weights[k][D:, :])
        hpre_ref[at, k * D : (k + 1) * D] = (
            grad_hidden * slope_ref[:, k * D : (k + 1) * D]
        ).astype(BF)
        grad_first = grad_first + dot_nt(hpre_ref[at, k * D : (k + 1) * D], weights[k][:D, :])
    grad_merged, first_gain, first_bias = norm_backward(grad_first, vec[2], first_kept)
    merged_ref[at, :] = (grad_merged + grad_sum).astype(BF)
    gains = jnp.zeros((D,), F32)
    biases = jnp.zeros((D,), F32)
    for scale in range(2):
        grad_branch = dot_nt(merged_ref[at, :], wm_ref[scale * D : (scale + 1) * D, :])
        grad, gain, bias = norm_backward(grad_branch, vec[0], stored[scale])
        gains, biases = gains + gain, biases + bias
        turn_ref[...] = grad
        for k, send_ref in zip(XOR, sends):
            send_ref[scale] = turn_ref[:, lane_at(t, k)].astype(BF)
    sums = (gains, biases, first_gain, first_bias, last_gain, last_bias)
    sums = jnp.concatenate([v[None, :] for v in sums] + [jnp.zeros((2, D), F32)], axis=0)
    sums_ref[...] = jnp.where(step == 0, sums, sums_ref[...] + sums)

    @pl.when(step == pl.num_programs(0) - 1)
    def _():
        wide = keep_ref.shape[1] // 2
        for i, (k, ref) in enumerate(zip(XOR, (keep_ref, keep_ref, give_ref, give_ref))):
            block = slice(i * D, (i + 1) * D)
            to = i % 2 * wide
            ref[:D, to : to + D] = dot_tn(first_ref[...], hpre_ref[:, block]).astype(BF)
            ref[D:, to : to + D] = dot_tn(hid_ref[:, block], feed_ref[...]).astype(BF)
            ref[:, to + D : to + wide] = dot_tn(
                pair_ref[...], merged_ref[:, lane_at(t, k)]
            ).astype(BF)


def rows_step(place, horizon, index, up_rows, x_full, cot_rows, vec, weights, merges):
    part_rows, width = cot_rows.shape[1:]
    steps = 3
    tile = part_rows // steps
    tall, wide = weights[0].shape[0], weights[0].shape[1] + width
    out = [
        shape_of(4, part_rows, width, kind=BF),
        *[shape_of(2, part_rows, width, kind=BF)] * 4,
        shape_of(tall, 2 * wide, kind=BF),
        shape_of(tall, 2 * wide, kind=BF),
        shape_of(8, D),
    ]
    one_way = pl.BlockSpec((4, tile, width), lambda i, place: (0, i, 0))
    two_way = pl.BlockSpec((2, tile, width), lambda i, place: (0, i, 0))
    once = lambda v: pl.BlockSpec(
        v.shape, lambda *_: (0,) * len(v.shape), pipeline_mode=pl.Buffered(1)
    )
    return pl.pallas_call(
        rows_kernel,
        grid_spec=pltpu.PrefetchScalarGridSpec(
            num_scalar_prefetch=1,
            grid=(steps,),
            in_specs=[
                scalars(),
                scalars(),
                pl.BlockSpec((tile, D), lambda i, place: (place[1] * steps + i, 0)),
                one_way,
                whole(vec),
                *[two_way] * 4,
                *[once(v) for v in weights + merges],
            ],
            out_specs=[one_way, *[two_way] * 4, *[whole(v) for v in out[5:]]],
            scratch_shapes=[
                pltpu.VMEM((2 * D, D), BF),
                pltpu.VMEM((tile, 4 * D), F32),
                pltpu.VMEM((tile, D), F32),
                pltpu.VMEM((part_rows, 4 * D), BF),
                pltpu.VMEM((part_rows, 4 * D), BF),
                pltpu.VMEM((part_rows, D), BF),
                pltpu.VMEM((part_rows, D), BF),
                pltpu.VMEM((part_rows, 2 * D), BF),
                pltpu.VMEM((part_rows, D), BF),
            ],
        ),
        out_shape=out,
        compiler_params=PARAMS,
        cost_estimate=cost(6 * part_rows * D * 10 * D, *weights, *merges, *out),
    )(place, horizon, index, x_full, cot_rows, vec, *up_rows, *weights, *merges)


def up_back_kernel(place_ref, *refs):
    held, (ua_ref, ub_ref, mid_ref, wa_ref, wb_ref) = refs[:4], refs[4:9]
    sums_ref, outs = refs[9], refs[10:14]
    grad_ref, kept_ref, rs_ref, cols_ref, part_ref = refs[14:]
    t = place_ref[1]
    part_rows = held[0].shape[1]
    rows = 4 * part_rows
    rs_ref[rows:, :] = jnp.zeros((rs_ref.shape[0] - rows, 128), F32)
    base = column = 0
    for scale, (stride, u_ref, w_ref) in enumerate(((SA, ua_ref, wa_ref), (SB, ub_ref, wb_ref))):
        count, wide = u_ref.shape
        for k, held_ref in zip(XOR, held):
            at = pl.ds(pl.multiple_of((t ^ k) * part_rows, part_rows), part_rows)
            value = held_ref[scale].astype(F32)
            rs_ref[at, :] = value
            kept_ref[at, :] = kept_ref[at, :] + value if scale else value
        for r in range(stride):
            up = u_ref[:, r * 128 : (r + 1) * 128]
            grad = rs_ref[pl.ds(r, count, stride=stride), :] * (1.0 - up * up)
            cols_ref[:count, r * 128 : (r + 1) * 128] = grad.astype(BF)
        grad = cols_ref[:count, :wide]
        part_ref[base : base + count, :] = dot_nt(grad, w_ref[...])
        grad_ref[:, column : column + wide] = dot_tn(mid_ref[base : base + count, :], grad).astype(BF)
        base += count
        column += wide
    part_ref[base:, :] = sums_ref[...]
    for k, out_ref in zip(XOR, outs):
        out_ref[...] = part_ref[:, lane_at(t, k)]


def up_backward(place, res, ua, ub, mid, weights, sums, tall):
    small = mid.shape[0]
    extra = small + sums.shape[0]
    _, part_rows, width = res[0].shape
    out = [
        *[shape_of(extra, width)] * 4,
        shape_of(D, ua.shape[1] + ub.shape[1], kind=BF),
        shape_of(4 * part_rows, width),
    ]
    return pl.pallas_call(
        up_back_kernel,
        in_specs=[scalars()] + [whole(v) for v in (*res, ua, ub, mid, *weights, sums)],
        out_specs=[whole(v) for v in out],
        out_shape=out,
        scratch_shapes=[
            pltpu.VMEM((tall, width), F32),
            pltpu.VMEM((max(ua.shape[0], ub.shape[0]), max(ua.shape[1], ub.shape[1])), BF),
            pltpu.VMEM((extra, D), F32),
        ],
        compiler_params=PARAMS,
        cost_estimate=cost(2 * small * D * out[4].shape[1], *res, ua, ub, mid, *weights, *out),
    )(place, *res, ua, ub, mid, *weights, sums)


def down_weight_kernel(counts, place_ref, plan_ref, index_ref, grad_ref, *refs):
    t = place_ref[1]
    several = grad_ref.shape[0]

    @pl.when(pl.program_id(0) == 0)
    def _():
        for sum_ref in refs[7:9]:
            sum_ref[...] = jnp.zeros_like(sum_ref)

    blocks = refs[:4]
    base = first = 0
    for count, out_ref in zip(counts, refs[7:9]):
        taps = out_ref.shape[0] // D
        for g in range(several):
            grad = grad_ref[g, base : base + count, :]
            for j in range(taps):
                at = slice(first + j * count, first + (j + 1) * count)
                x = jnp.concatenate([v[g, at, :] for v in blocks], axis=1)
                part = dot_tn(x, grad)
                for i, k in enumerate(XOR):
                    to = pl.ds(pl.multiple_of(j * D + (t ^ k) * 128, 128), 128)
                    out_ref[to, :] = out_ref[to, :] + part[i * 128 : (i + 1) * 128]
        base += count
        first += taps * count
    held_ref = refs[-1]
    held_ref[index_ref[pl.program_id(0)]] = grad_ref[0, base:, :].astype(F32)

    @pl.when(pl.program_id(0) == pl.num_programs(0) - 1)
    def _():
        for i in range(2):
            out_ref, sum_ref = refs[4 + i], refs[7 + i]
            at = pl.ds(pl.multiple_of(plan_ref[4 + i], 8), out_ref.shape[0])
            out_ref[...] = sum_ref[at, :]
        total = held_ref[0]
        for i in range(1, held_ref.shape[0]):
            total = total + held_ref[i]
        refs[6][...] = total


def down_weight_grad(place, plan, index, grad_all, blocks, counts, taps, held):
    groups, small, width = grad_all.shape
    sums = [pltpu.VMEM((n * D, width), F32) for n in taps]
    rest = small - sum(counts)
    sums.append(pltpu.VMEM((groups, rest, width), F32))
    out = [shape_of(n, width) for n in held] + [shape_of(rest, width)]
    block = lambda v: pl.BlockSpec((1,) + v.shape[1:], lambda i, place, plan, index: (index[i], 0, 0))
    return pl.pallas_call(
        partial(down_weight_kernel, counts),
        grid_spec=pltpu.PrefetchScalarGridSpec(
            num_scalar_prefetch=3,
            grid=(groups,),
            in_specs=[pl.BlockSpec((1, small, width), lambda i, *_: (i, 0, 0))]
            + [block(v) for v in blocks],
            out_specs=[whole(v) for v in out],
            scratch_shapes=sums,
        ),
        out_shape=out,
        compiler_params=PARAMS,
        cost_estimate=cost(8 * blocks[0].size * 4 * width // 2, grad_all, *blocks),
    )(place, plan, index, grad_all, *blocks)


def down_input_kernel(count, place_ref, index_ref, grad_ref, *refs):
    parts, refs = refs[:count], refs[count:]
    outs, (gx_ref, wa_ref, wb_ref) = refs[:4], refs[4:]
    t = place_ref[1]
    rows = outs[0].shape[0]
    assemble(wa_ref, wb_ref, index_ref, parts)
    base = 0
    for stride, weight in ((SA, wa_ref), (SB, wb_ref)):
        count = -(-rows // stride // 16) * 16
        grad = grad_ref[base : base + count, :]
        for r in range(stride):
            at = pl.ds(r, count, stride=stride)
            part = dot_nt(grad, weight[r * D : (r + 1) * D, :])
            for j in range(4):
                lane = slice(j * 128, (j + 1) * 128)
                if base:
                    gx_ref[j, at, :] = gx_ref[j, at, :] + part[:, lane]
                else:
                    gx_ref[j, at, :] = part[:, lane]
        base += count
    for k, out_ref in zip(XOR, outs):
        out_ref[...] = gx_ref[t ^ k, :rows, :].astype(BF)


def down_input_grad(place, index, grad, parts, rows, tall):
    width = grad.shape[1]
    out = [shape_of(rows, width, kind=BF)] * 4
    return pl.pallas_call(
        partial(down_input_kernel, len(parts)),
        in_specs=[scalars()] * 2 + [whole(v) for v in (grad, *parts)],
        out_specs=[whole(v) for v in out],
        out_shape=out,
        scratch_shapes=[
            pltpu.VMEM((4, tall, 128), F32),
            pltpu.VMEM((SA * D, width), BF),
            pltpu.VMEM((SB * D, width), BF),
        ],
        compiler_params=PARAMS,
        cost_estimate=cost(4 * rows * D * width, grad, *parts, *out),
    )(place, index, grad, *parts)


def body(
    signal,
    horizon,
    down_a,
    iso_a,
    up_a,
    down_b,
    iso_b,
    up_b,
    merge_w,
    ff_in,
    ff_out,
    norm_gain,
    norm_bias,
    first_gain,
    first_bias,
    last_gain,
    last_bias,
    cotangent,
):
    row_count, col_count = signal.shape
    part_rows = row_count // 4
    counts = (row_count // SA, -(-row_count // SB // 16) * 16)
    small = counts[0] + counts[1]
    tall = max(counts[0] * SA, counts[1] * SB)
    spans = ((counts[0], MA), (counts[1], MB))
    t = lax.axis_index("tensor")
    group = lax.axis_index("dp")
    place = jnp.stack([group, t]).astype(jnp.int32)
    count = lax.axis_size("dp")
    index = own_row(ring_places(count))
    taps_a, *taps_plan_a = tap_plan(iso_a.shape[0], MA, count)
    taps_b, *taps_plan_b = tap_plan(iso_b.shape[0], MB, count)
    down_offsets = [
        [i * v.shape[0] - first * D for i, first in enumerate(positions(v.shape[0], stride, count)[1])]
        for v, stride in ((down_a, SA), (down_b, SB))
    ]
    table = [taps_plan_a[1], taps_plan_b[1], taps_plan_a[0], taps_plan_b[0], *down_offsets]
    plan = own_row(np.array(table, np.int32).T)

    vec_own = jnp.stack(
        [norm_gain, norm_bias, first_gain, first_bias, last_gain, last_bias, last_bias, last_bias]
    )
    split = [lax.reduce_precision(vec_own, 8, 7)]
    split.append(lax.reduce_precision(vec_own - split[0], 8, 7))
    split.append(vec_own - split[0] - split[1])
    split.append(jnp.zeros_like(vec_own))
    x_own = jnp.concatenate([signal] + [v.astype(BF) for v in split], axis=0)
    parts, x_blocks = ring_list(
        jnp.concatenate([down_a, down_b, merge_w], axis=0),
        halves=True,
        beside=(
            lambda _: [swap(x_own, 2)],
            lambda held: [swap(x_own, 1), swap(held[0], 1)],
        ),
    )
    x_blocks = [x_own] + x_blocks

    ff_own, x_blocks[1] = together(jnp.concatenate([ff_in, ff_out], axis=0), x_blocks[1])
    ff_blocks = four(ff_own)
    up_held_a, up_held_b, parts[-1] = together(
        up_a.reshape(up_a.shape[0], -1), up_b.reshape(up_b.shape[0], -1), parts[-1]
    )
    w_up_a = lax.all_gather(up_held_a, "dp", axis=0, tiled=True)
    w_up_b = lax.all_gather(up_held_b, "dp", axis=0, tiled=True)
    act, low, x_full, x_send, vec = down_forward(
        place, index, x_blocks, parts, counts, small, tall
    )
    iso_held = after((iso_a, iso_b), low)
    wide_a, wide_b = tap_columns(place, plan, *iso_held, (taps_a, taps_b))

    low_across = swap(low, 2)
    (cot_held,) = after((cotangent,), low_across)
    cot_rows = lax.all_to_all(
        cot_held.reshape(4, part_rows, col_count), "tensor", 0, 0, tiled=True
    )
    pair_all = ring_stack(jnp.concatenate([low, low_across], axis=1))
    (pair_all,) = after((pair_all,), cot_rows, w_up_a, ff_blocks[1])
    far_all = swap(pair_all, 1)
    merge_own = jnp.stack([v[down_a.shape[0] + down_b.shape[0] :] for v in parts])
    (merge_own,) = after((merge_own,), pair_all)
    merge_blocks = four(merge_own)
    iso_part = iso_forward(plan, index, pair_all, far_all, wide_a, wide_b, spans)
    iso_pre, w_up_b = together(exchange_sum(iso_part), w_up_b)
    *send, up_act_a, up_act_b, middle, normed, inv_std, iso_own = up_forward(
        place, four(iso_pre), pair_all, far_all, vec, (w_up_a, w_up_b), counts, part_rows, tall
    )
    (x_send,) = after((x_send,), iso_pre)
    x_pos = lax.all_to_all(x_send, "dp", 0, 0, tiled=True)
    up_rows = exchange(send)
    last, *out = rows_step(
        place, horizon, index, up_rows, x_full, cot_rows, vec, ff_blocks, merge_blocks
    )
    res_send, (keep_w, give_w, sums) = out[:4], out[4:]
    x_pos, *res_send = together(x_pos, *res_send)
    res = exchange(res_send)
    give_w, res[2] = together(give_w, res[2])
    sum_w = (keep_w.astype(F32) + swap(give_w, 1).astype(F32)).astype(BF)
    sum_w = lax.psum_scatter(sum_w, "dp", scatter_dimension=0, tiled=True)

    *mid_parts, grad_up, resid = up_backward(
        place, res, up_act_a, up_act_b, middle, (w_up_a, w_up_b), sums, tall
    )
    sum_up = lax.psum_scatter(grad_up, "dp", scatter_dimension=0, tiled=True)
    near = mid_parts[0] + swap(mid_parts[2], 1)
    far = mid_parts[1] + swap(mid_parts[3], 1)
    crossed = swap(jnp.concatenate([far, near], axis=1).astype(BF), 2).astype(F32)
    keep = jnp.concatenate([near, far], axis=1) + crossed
    grad_middle = jnp.concatenate([keep, swap(keep, 1)], axis=1)
    last, x_pos, grad_middle = together(last, x_pos, grad_middle)
    sums = grad_middle[small:, :col_count]
    grad_middle = grad_middle[:small]
    series_out = lax.all_to_all(last, "tensor", 0, 0, tiled=True)
    x_pos = four(x_pos)
    x_gain = jnp.concatenate(xor_order(lanes(vec[:1])), axis=1)
    grad_inner, gain_mid, bias_mid = norm_backward(grad_middle, x_gain, (normed, inv_std[:, :1]))
    grad_inner = grad_inner[:, :col_count]
    grad_ipre_all = ring_stack((grad_inner * (1.0 - iso_own * iso_own)).astype(BF))
    grad_iso_a, grad_iso_b, *back = iso_backward(
        place, plan, index, grad_ipre_all, pair_all, far_all, wide_a, wide_b, spans,
        (iso_a.shape[0], iso_b.shape[0]),
    )
    series_out, *back = together(series_out, *back)
    series_out = series_out.reshape(row_count, col_count)
    own_back = own_sum(back)
    sum_w, own_back = together(sum_w, own_back)
    wide = D + col_count
    sum_w = sum_w[:, :wide].astype(F32) + swap(sum_w[:, wide:], 2).astype(F32)
    sum_merge = sum_w[:, D:]
    grad_down = exchange_sum(own_back)
    grad_dpre = ((grad_down + grad_inner) * (1.0 - act * act)).astype(BF)
    x_parts = down_input_grad(place, index, grad_dpre, parts, row_count, tall)
    sums = sums + jnp.pad(
        jnp.stack([gain_mid[:col_count], bias_mid[:col_count]]), ((0, 6), (0, 0))
    )
    sums = jnp.pad(sums, ((0, 8), (0, 0))).astype(BF)
    grad_dpre_all = ring_stack(jnp.concatenate([grad_dpre, sums], axis=0))
    ff_total = lax.all_gather(sum_w[:, :D].astype(BF), "dp", axis=0, tiled=True)
    grad_dpre_all, ff_total = together(grad_dpre_all, ff_total)
    sum_down_a, sum_down_b, sums = down_weight_grad(
        place, plan, index, grad_dpre_all, x_pos, counts,
        [positions(v.shape[0], n, count)[0] for v, n in ((down_a, SA), (down_b, SB))],
        (down_a.shape[0], down_b.shape[0]),
    )
    grad_input = own_sum(x_parts) + resid

    ff_total = ff_total.astype(F32)
    sum_up = sum_up.astype(F32)
    sum_up_a = sum_up[:, : SA * col_count].reshape(up_a.shape)
    sum_up_b = sum_up[:, SA * col_count :].reshape(up_b.shape)
    return (
        series_out,
        grad_input,
        sum_down_a,
        grad_iso_a,
        sum_up_a,
        sum_down_b,
        grad_iso_b,
        sum_up_b,
        sum_merge,
        ff_total[:D],
        ff_total[D:],
        sums[0],
        sums[1],
        sums[2],
        sums[3],
        sums[4],
        sums[5],
    )


def solution(mesh):
    in_specs = (
        P("dp", "tensor"),
        P("dp"),
        P("dp", "tensor"),
        P("dp", "tensor"),
        P("dp", None, "tensor"),
        P("dp", "tensor"),
        P("dp", "tensor"),
        P("dp", None, "tensor"),
        P("dp", "tensor"),
        P(None, "tensor"),
        P("tensor", None),
        P("tensor"),
        P("tensor"),
        P("tensor"),
        P("tensor"),
        P("tensor"),
        P("tensor"),
        P("dp", "tensor"),
    )
    out_specs = (
        P("dp", "tensor"),
        P("dp", "tensor"),
        P("dp", "tensor"),
        P("dp", "tensor"),
        P("dp", None, "tensor"),
        P("dp", "tensor"),
        P("dp", "tensor"),
        P("dp", None, "tensor"),
        P("dp", "tensor"),
        P(None, "tensor"),
        P("tensor", None),
        P("tensor"),
        P("tensor"),
        P("tensor"),
        P("tensor"),
        P("tensor"),
        P("tensor"),
    )
    return jax.shard_map(body, mesh=mesh, in_specs=in_specs, out_specs=out_specs, check_vma=False)
```
